128 devices in a mesh: grp: 8 (over z_lo, x), obs: 16 (over y, z_hi, core).
Axes of the slice: x: 4, y: 4, z: 4 (z_hi: 2, z_lo: 2; z = z_hi * 2 + z_lo), core: 2. Of those that a mesh axis runs over, the one named last changes fastest.
Arguments:
- signals: bfloat16 [4, 256, 131072], P(None, None, ('grp', 'obs')), may hold values from -6 to 6
- patch_count: int32 [128], P(('grp', 'obs')), may hold values from 0 to 8, as said below
- patch_place: int32 [1024], P(('grp', 'obs')), may hold values from 0 to 63, as said below
- face_geom: float32 [4, 65536], P(None, ('grp', 'obs')), may hold values from -3.5 to 30, as said below
- obs_pos: float32 [3, 4096], P(None, 'obs'), may hold values from -60 to 60, as said below
Outputs:
- pressure: float32 [16, 4096], P('grp', 'obs')
The draws below stay inside these ranges and needn't reach their ends.
Inputs may be any that keep to these rules, and one draw needn't show every extreme that they name: `patch_count`: each partition holds 0 to 8 live patches; in every face group the counts sum to 64 and some partition holds exactly 8. `patch_place`: A live slot names owner o and patch j of the partition's group as o * 4 + j; within a group every such value is named by exactly one live slot, so every owner receives exactly 4 patches; no partition holds two live patches of the same owner. Slots beyond the count hold arbitrary values in the range. `face_geom`: faces lie on a surface around the first coordinate's axis: the first coordinate between 0 and 30, the distance from that axis between 2 and 3.5; the area lies between 0.5 and 10. `obs_pos`: every observer lies 25 to 60 from the anchor (0, 0, 0) and 8 or more from the first coordinate's axis.
All inputs are finite; a program needn't handle non-finite values.
Results may differ from the reference program's by a relative error of at most 0.004.
Values may be sent and summed in bfloat16 or wider, within the bound.
No kernel may reach another device: no remote copies, remote signals or barrier semaphores. Data moves between devices by JAX's collectives and lax.ppermute only.
A program may use at most 64 MiB of HBM per device.

```python
import math
import jax
import jax.numpy as jnp
from jax import lax

SAMPLES = 256
NFREQ = 8
NSIG = 4
PATCH = 128
MAXP = 8
PER_OWN = 4
GROUPS = 8
OWNERS = 16
ROWS_DEV = 1024
ROWS = 131072
FACES = 65536
OBSERVERS = 4096


def draw_tables(key):

    def one_group(group_key):
        member = jnp.arange(OWNERS, dtype=jnp.int32)
        level = PER_OWN - member // 2 % (PER_OWN + 1)
        signed = 1 - 2 * (member % 2)
        counts = PER_OWN + signed * level
        counts = jax.random.permutation(jax.random.fold_in(group_key, 1), counts)
        starts = jnp.cumsum(counts) - counts
        slot_index = jnp.arange(MAXP, dtype=jnp.int32)
        position = starts[:, None] + slot_index[None, :]
        order = jax.random.permutation(jax.random.fold_in(group_key, 2), OWNERS).astype(jnp.int32)
        place = order[position % OWNERS] * PER_OWN + position // OWNERS
        filler = jax.random.randint(jax.random.fold_in(group_key, 3), (OWNERS, MAXP), 0, PER_OWN * OWNERS)
        place = jnp.where(slot_index[None, :] < counts[:, None], place, filler)
        return (counts.astype(jnp.int32), place.reshape(-1).astype(jnp.int32))
    group_keys = jax.vmap(lambda number: jax.random.fold_in(jax.random.fold_in(key, 17), number))(jnp.arange(GROUPS))
    counts, places = jax.vmap(one_group)(group_keys)
    return (counts.reshape(-1).astype(jnp.int32), places.reshape(-1).astype(jnp.int32))


def draw_patch_count(key, part):
    return draw_tables(key)[0]


def draw_patch_place(key, part):
    return draw_tables(key)[1]


def draw_face_geom(key, part):
    key_axial = jax.random.fold_in(key, 31)
    key_radial = jax.random.fold_in(key, 33)
    key_around = jax.random.fold_in(key, 34)
    key_area = jax.random.fold_in(key, 32)
    axial = jax.random.uniform(key_axial, (FACES,), jnp.float32, 0.0, 30.0)
    radial = jax.random.uniform(key_radial, (FACES,), jnp.float32, 2.0, 3.5)
    beside_all = jax.random.uniform(key_around, (FACES,), jnp.float32, 0.0, 2.0 * math.pi)
    position = jnp.stack([axial, radial * jnp.cos(beside_all), radial * jnp.sin(beside_all)], axis=0)
    low_area = 1.0
    area = jnp.exp(jax.random.uniform(key_area, (1, FACES), jnp.float32, math.log(low_area), math.log(10.0)))
    return jnp.concatenate([position, area], axis=0).astype(jnp.float32)


def draw_obs_pos(key, part):
    key_radius = jax.random.fold_in(key, 41)
    key_polar = jax.random.fold_in(key, 42)
    key_azim = jax.random.fold_in(key, 43)
    radius = jax.random.uniform(key_radius, (OBSERVERS,), jnp.float32, 25.0, 60.0)
    polar = jax.random.uniform(key_polar, (OBSERVERS,), jnp.float32, 0.35, math.pi - 0.35)
    azimuth = jax.random.uniform(key_azim, (OBSERVERS,), jnp.float32, 0.0, 2.0 * math.pi)
    rows_out = [radius * jnp.cos(polar), radius * jnp.sin(polar) * jnp.cos(azimuth), radius * jnp.sin(polar) * jnp.sin(azimuth)]
    return jnp.stack(rows_out, axis=0).astype(jnp.float32)


def block_scale(rng, dims, cuts, least, largest):
    loudness, own = 1.0, jax.random.fold_in(rng, 6)
    for axis_at, blocks in cuts:
        steps = jnp.exp(jax.random.uniform(jax.random.fold_in(own, axis_at), (blocks,), jnp.float32, least / len(cuts), largest / len(cuts)))
        loudness = loudness * jnp.repeat(steps, dims[axis_at] // blocks).reshape([-1 if axis == axis_at else 1 for axis in range(len(dims))])
    return loudness


def bell_draw(rng, extent, scale, bound, cuts=(), kind=jnp.bfloat16):
    values = jax.random.normal(rng, extent, jnp.float32) * scale
    if len(cuts) > 0:
        values = block_scale(rng, extent, cuts, -0.22, 0.18) * values
    return jnp.clip(values, min=-bound, max=bound).astype(kind)


def setup_inputs(seed: int = 0) -> dict:
    key_of = jax.random.split(jax.random.key(seed), 6)
    signals = bell_draw(key_of[0], (NSIG, SAMPLES, ROWS), 1.0, 6.0, ((2, 128),))
    patch_count = draw_patch_count(jax.random.fold_in(key_of[5], 71), 0)
    patch_place = draw_patch_place(jax.random.fold_in(key_of[5], 71), 0)
    face_geom = draw_face_geom(jax.random.fold_in(key_of[5], 71), 0)
    obs_pos = draw_obs_pos(jax.random.fold_in(key_of[5], 71), 0)
    return dict(signals=signals, patch_count=patch_count, patch_place=patch_place, face_geom=face_geom, obs_pos=obs_pos)


omega_step = 0.5
four_pi = 4.0 * math.pi

def spectral_basis(samples, freq_count):
    sample_idx = jnp.arange(samples, dtype=jnp.float32)
    harmonic = jnp.arange(1, freq_count + 1, dtype=jnp.float32)
    angles = 2.0 * math.pi / samples * (sample_idx[:, None] * harmonic[None, :])
    window = (0.5 - 0.5 * jnp.cos(2.0 * math.pi / samples * sample_idx)) * math.sqrt(8.0 / (3.0 * samples))
    table = jnp.concatenate([window[:, None] * jnp.cos(angles), -window[:, None] * jnp.sin(angles)], axis=1)
    return table.astype(jnp.bfloat16)

def pressure_tiles(observers, spectra, geometry):
    freq_count = spectra.shape[0] // 8
    wavenumber = omega_step * jnp.arange(1, freq_count + 1, dtype=jnp.float32)
    values = spectra.astype(jnp.float32).reshape(4, 2, freq_count, spectra.shape[1])
    separation = observers[:, :, None] - geometry[:3, None, :]
    dist_sq = lax.optimization_barrier(jnp.sum(separation * separation, axis=0))
    distance = jnp.sqrt(dist_sq)
    inv_sq = 1.0 / dist_sq
    load_re = jnp.zeros((freq_count,) + dist_sq.shape, jnp.float32)
    load_im = jnp.zeros((freq_count,) + dist_sq.shape, jnp.float32)
    for coord in range(3):
        load_re = load_re + values[1 + coord, 0][:, None, :] * separation[coord][None]
        load_im = load_im + values[1 + coord, 1][:, None, :] * separation[coord][None]
    dip_re = load_re * inv_sq[None]
    dip_im = load_im * inv_sq[None]
    omega_grid = wavenumber[:, None, None]
    phase = omega_grid * distance[None]
    mono_re = values[0, 0][:, None, :]
    mono_im = values[0, 1][:, None, :]
    bracket_re = -omega_grid * mono_im + dip_re - phase * dip_im
    bracket_im = omega_grid * mono_re + dip_im + phase * dip_re
    amplitude = (geometry[3][None, :] / (four_pi * distance))[None]
    green_re = amplitude * jnp.cos(phase)
    green_im = -amplitude * jnp.sin(phase)
    press_re = lax.optimization_barrier(jnp.sum(green_re * bracket_re - green_im * bracket_im, axis=2))
    press_im = lax.optimization_barrier(jnp.sum(green_re * bracket_im + green_im * bracket_re, axis=2))
    return jnp.concatenate([press_re, press_im], axis=0)

def reference(signals, patch_count, patch_place, face_geom, obs_pos):
    dft_basis = spectral_basis(SAMPLES, NFREQ).astype(jnp.float32)
    partitions = GROUPS * OWNERS
    part_blocks = signals.reshape(NSIG, SAMPLES, partitions, ROWS_DEV).transpose(2, 0, 1, 3)

    def transform(part_block):
        spectrum = jnp.einsum('sti,tc->sci', part_block.astype(jnp.float32), dft_basis, precision=lax.Precision.HIGHEST)
        return spectrum.astype(jnp.bfloat16)
    row_spectra = lax.map(transform, part_blocks)
    channels = NSIG * 2 * NFREQ
    row_spectra = row_spectra.reshape(partitions, channels, MAXP, PATCH).transpose(0, 2, 1, 3)
    row_spectra = row_spectra.reshape(partitions * MAXP, channels, PATCH)
    slot_index = jnp.arange(partitions * MAXP, dtype=jnp.int32)
    partition_of = slot_index // MAXP
    is_live = slot_index % MAXP < patch_count[partition_of]
    group_of = partition_of // OWNERS
    target = jnp.where(is_live, group_of * (OWNERS * PER_OWN) + patch_place, partitions * PER_OWN).astype(jnp.int32)
    placed = jnp.zeros((partitions * PER_OWN, channels, PATCH), row_spectra.dtype)
    placed = placed.at[target].set(row_spectra, mode='drop')
    face_spectra = placed.transpose(1, 0, 2).reshape(channels, FACES)
    block_len = math.gcd(FACES, 256)
    step_count = FACES // block_len
    spec_blocks = face_spectra.reshape(channels, step_count, block_len).transpose(1, 0, 2)
    geom_blocks = face_geom.reshape(4, step_count, block_len).transpose(1, 0, 2)

    def add_block(running, pieces):
        return (running + pressure_tiles(obs_pos, pieces[0], pieces[1]), None)
    zero_sum = jnp.zeros((2 * NFREQ, OBSERVERS), jnp.float32)
    pressure, _ = lax.scan(add_block, zero_sum, (spec_blocks, geom_blocks))
    return pressure
```

```python
import math

import jax
import jax.numpy as jnp
import numpy as np
from jax import lax
from jax.experimental import pallas as pl
from jax.experimental.pallas import tpu as pltpu
from jax.sharding import PartitionSpec as P

SAMPLES = 256
NFREQ = 8
NSIG = 4
PATCH = 128
MAXP = 8
PER_OWN = 4
FACES_OWN = 512
CHANNELS = NSIG * 2 * NFREQ
ROWS_MSG = 96
OBS_ROW = 64
TAIL_ROW = 80
OBS_TILE = 256
CHUNK = 64
CHUNKS = FACES_OWN // CHUNK
TERMS = 32
CENTER_X = 15.0

COS_COEFS = (
    0.9999992107823207,
    -19.73898035576387,
    64.92865742102978,
    -85.27162153426406,
    58.790492119980826,
    -21.071105627415147,
)
SIN_COEFS = (
    6.283184916495429,
    -41.34158923268831,
    81.59994332977428,
    -76.61447253115396,
    41.342882354135696,
    -12.471243534350362,
)


def spectral_basis():
    t = np.arange(SAMPLES, dtype=np.float64)
    m = np.arange(1, NFREQ + 1, dtype=np.float64)
    angles = 2.0 * math.pi / SAMPLES * (t[:, None] * m[None, :])
    window = (0.5 - 0.5 * np.cos(2.0 * math.pi / SAMPLES * t)) * math.sqrt(8.0 / (3.0 * SAMPLES))
    table = np.concatenate(
        [window[:, None] * np.cos(angles), -window[:, None] * np.sin(angles)], axis=1
    )
    return jnp.asarray(table.T.astype(np.float32)).astype(jnp.bfloat16)


def pack_kernel(count_ref, place_ref, basis_ref, signals_ref, obs_ref, out_ref):
    sig = pl.program_id(0)

    @pl.when(sig == 0)
    def _():
        x = obs_ref[...]
        hi = x.astype(jnp.bfloat16).astype(jnp.float32)
        rest = x - hi
        mid = rest.astype(jnp.bfloat16).astype(jnp.float32)
        low = rest - mid
        rows = []
        for part in (hi, mid, low):
            for c in range(3):
                for h in range(2):
                    rows.append(part[c : c + 1, h * PATCH : (h + 1) * PATCH])
        head = jnp.concatenate(rows[:16], axis=0).astype(jnp.bfloat16)
        tail = jnp.concatenate(
            rows[16:] + [jnp.zeros((14, PATCH), jnp.float32)], axis=0
        )
        out_ref[...] = jnp.zeros_like(out_ref)
        for o in range(out_ref.shape[0]):
            out_ref[o, OBS_ROW:TAIL_ROW, :] = head
            out_ref[o, TAIL_ROW:, :] = tail.astype(jnp.bfloat16)
        row_id = lax.broadcasted_iota(jnp.int32, (16, PATCH), 0)
        for j in range(MAXP):
            place = place_ref[j]
            owner = place // PER_OWN
            part_no = (place % PER_OWN + 1).astype(jnp.float32)

            @pl.when(j < count_ref[0])
            def _():
                out_ref[owner, TAIL_ROW:, :] = jnp.where(row_id < 2, tail, part_no).astype(
                    jnp.bfloat16
                )

    spec = jnp.dot(
        basis_ref[...], signals_ref[0], preferred_element_type=jnp.float32
    ).astype(jnp.bfloat16)
    row0 = pl.multiple_of(sig * 16, 16)
    for j in range(MAXP):

        @pl.when(j < count_ref[0])
        def _():
            owner = place_ref[j] // PER_OWN
            out_ref[owner, pl.ds(row0, 16), :] = spec[:, j * PATCH : (j + 1) * PATCH]


def pack(signals, patch_count, patch_place, obs_pos, owners):
    return pl.pallas_call(
        pack_kernel,
        grid=(NSIG,),
        in_specs=[
            pl.BlockSpec(memory_space=pltpu.SMEM),
            pl.BlockSpec(memory_space=pltpu.SMEM),
            pl.BlockSpec((2 * NFREQ, SAMPLES), lambda s: (0, 0)),
            pl.BlockSpec((1, SAMPLES, MAXP * PATCH), lambda s: (s, 0, 0)),
            pl.BlockSpec(obs_pos.shape, lambda s: (0, 0)),
        ],
        out_specs=pl.BlockSpec((owners, ROWS_MSG, PATCH), lambda s: (0, 0, 0)),
        out_shape=jax.ShapeDtypeStruct((owners, ROWS_MSG, PATCH), jnp.bfloat16),
        name="pack",
    )(patch_count, patch_place, spectral_basis(), signals, obs_pos)


def horner(coefs, z):
    acc = jnp.full_like(z, coefs[-1])
    for c in coefs[-2::-1]:
        acc = acc * z + c
    return acc


def face_matrices(t, j, obs_ref, face_ref, g_ref):
    x = [obs_ref[t, c : c + 1, :] for c in range(3)]
    for group in range(CHUNK // 16):
        f0 = pl.multiple_of(j * CHUNK + group * 16, 16)
        cols = [face_ref[c, pl.ds(f0, 16), :] for c in range(4)]
        y = [jnp.concatenate([col, col], axis=1) for col in cols]
        dx = x[0] - y[0]
        dy = x[1] - y[1]
        dz = x[2] - y[2]
        r2 = dx * dx + dy * dy + dz * dz
        inv = lax.rsqrt(r2)
        r = r2 * inv
        turns = r * (0.25 / math.pi)
        frac = turns - jnp.floor(turns + 0.5)
        z = frac * frac
        cos1 = horner(COS_COEFS, z)
        sin1 = horner(SIN_COEFS, z) * frac
        amp = y[3] * inv * (inv * inv)
        two_cos = cos1 + cos1
        c_old, s_old = amp, None
        c_now, s_now = amp * cos1, amp * sin1
        for m in range(NFREQ):
            if m == 1:
                c_old, c_now = c_now, two_cos * c_now - c_old
                s_old, s_now = s_now, two_cos * s_now
            elif m > 1:
                c_old, c_now = c_now, two_cos * c_now - c_old
                s_old, s_now = s_now, two_cos * s_now - s_old
            g_ref[m, group * 16 : group * 16 + 16, :] = (c_now * r).astype(jnp.bfloat16)
            g_ref[m, CHUNK + group * 16 : CHUNK + group * 16 + 16, :] = (s_now * r).astype(
                jnp.bfloat16
            )
            g_ref[m, 2 * CHUNK + group * 16 : 2 * CHUNK + group * 16 + 16, :] = c_now.astype(
                jnp.bfloat16
            )
            g_ref[m, 3 * CHUNK + group * 16 : 3 * CHUNK + group * 16 + 16, :] = s_now.astype(
                jnp.bfloat16
            )


def face_products(j, w_ref, g_ref, acc_ref):
    first = j == 0
    for m in range(NFREQ):
        part = jnp.dot(w_ref[j, m], g_ref[m], preferred_element_type=jnp.float32)
        acc_ref[m] = jnp.where(first, 0.0, acc_ref[m]) + part


def finish_tile(t, obs_ref, acc_ref, out_ref):
    x = [obs_ref[t, c : c + 1, :] for c in range(3)]
    xx = x[0] * x[0] + x[1] * x[1] + x[2] * x[2]
    for m in range(NFREQ):
        k = 0.5 * (m + 1)
        for part in range(2):
            row = lambda n: acc_ref[m, 2 * n + part : 2 * n + part + 1, :]
            total = row(0) + row(1) + xx * row(2)
            for c in range(3):
                total = total + x[c] * (row(3 + c) + row(6 + c))
            at = part * NFREQ + m
            out_ref[t, at : at + 1, :] = total * (k / (4.0 * math.pi))


def pressure_kernel(w_ref, geom_ref, obs_ref, out_ref, face_ref, ga_ref, gb_ref, acc_ref):
    tiles = obs_ref.shape[0]
    geom = jnp.concatenate([geom_ref[...], jnp.zeros((4, FACES_OWN), jnp.float32)], axis=0)
    cols = geom.T
    for c in range(4):
        face_ref[c] = jnp.broadcast_to(cols[:, c : c + 1], (FACES_OWN, PATCH))

    def pair(t, jj):
        face_matrices(t, 2 * jj, obs_ref, face_ref, ga_ref)
        return None

    def step(i, carry):
        t = i // (CHUNKS // 2)
        jj = i % (CHUNKS // 2)
        t_old = jnp.where(jj == 0, t - 1, t)
        j_old = jnp.where(jj == 0, CHUNKS - 1, 2 * jj - 1)
        face_matrices(t, 2 * jj, obs_ref, face_ref, ga_ref)
        face_products(j_old, w_ref, gb_ref, acc_ref)

        @pl.when(jnp.logical_and(jj == 0, t > 0))
        def _():
            finish_tile(t_old, obs_ref, acc_ref, out_ref)

        face_matrices(t, 2 * jj + 1, obs_ref, face_ref, gb_ref)
        face_products(2 * jj, w_ref, ga_ref, acc_ref)
        return carry

    lax.fori_loop(0, tiles * (CHUNKS // 2), step, 0)
    face_products(CHUNKS - 1, w_ref, gb_ref, acc_ref)
    finish_tile(tiles - 1, obs_ref, acc_ref, out_ref)


def partial_pressure(weights, geom, observers):
    tiles = observers.shape[0]
    return pl.pallas_call(
        pressure_kernel,
        in_specs=[pl.BlockSpec(memory_space=pltpu.VMEM)] * 3,
        out_specs=pl.BlockSpec(memory_space=pltpu.VMEM),
        out_shape=jax.ShapeDtypeStruct((tiles, 2 * NFREQ, OBS_TILE), jnp.float32),
        scratch_shapes=[
            pltpu.VMEM((4, FACES_OWN, PATCH), jnp.float32),
            pltpu.VMEM((NFREQ, 4 * CHUNK, OBS_TILE), jnp.bfloat16),
            pltpu.VMEM((NFREQ, 4 * CHUNK, OBS_TILE), jnp.bfloat16),
            pltpu.VMEM((NFREQ, TERMS, OBS_TILE), jnp.float32),
        ],
        compiler_params=pltpu.CompilerParams(vmem_limit_bytes=48 * 1024 * 1024),
        name="pressure",
    )(weights, geom, observers)


def face_weights(spec, geom):
    k = (0.5 * jnp.arange(1, NFREQ + 1, dtype=jnp.float32))[:, None]
    y = geom[:3]
    yy = jnp.sum(y * y, axis=0)[None]
    qr, qi = spec[0, 0], spec[0, 1]
    lr = [spec[1 + c, 0] for c in range(3)]
    li = [spec[1 + c, 1] for c in range(3)]
    lyr = sum(lr[c] * y[c][None] for c in range(3))
    lyi = sum(li[c] * y[c][None] for c in range(3))
    zero = jnp.zeros_like(qr)

    def four(load_r, load_i, mono):
        re = (-load_i, load_r, load_r / k - mono * qi, load_i / k + mono * qr)
        im = (load_r, load_i, load_i / k + mono * qr, -load_r / k + mono * qi)
        return [jnp.stack(re), jnp.stack(im)]

    def split(v):
        hi = lax.reduce_precision(v, 8, 7)
        return hi, v - hi

    base = [split(v) for v in four(-lyr, -lyi, yy)]
    load = [[split(v) for v in four(lr[c], li[c], -2.0 * y[c][None])] for c in range(3)]
    square = four(zero, zero, jnp.ones_like(yy))
    rows = [base[p][0] for p in range(2)] + [base[p][1] for p in range(2)] + square
    rows += [load[c][p][0] for c in range(3) for p in range(2)]
    rows += [load[c][p][1] for c in range(3) for p in range(2)]
    rows += [jnp.zeros_like(rows[0])] * (TERMS - len(rows))
    w = jnp.stack(rows)
    w = w.reshape(TERMS, 4, NFREQ, CHUNKS, CHUNK).transpose(3, 2, 0, 1, 4)
    return w.reshape(CHUNKS, NFREQ, TERMS, 4 * CHUNK).astype(jnp.bfloat16)


def local(signals, patch_count, patch_place, face_geom, obs_pos):
    owners = lax.axis_size("obs")
    groups = lax.axis_size("grp")
    outgoing = pack(signals, patch_count, patch_place, obs_pos, owners)
    arrived = lax.all_to_all(outgoing, "obs", split_axis=0, concat_axis=0, tiled=True)
    header = arrived[:, ROWS_MSG - 1, 0]
    owned = (header[:, None] == jnp.arange(1, PER_OWN + 1).astype(jnp.bfloat16)[None, :]).astype(
        jnp.bfloat16
    )
    spec = jnp.einsum(
        "oj,okp->kjp", owned, arrived[:, :CHANNELS], preferred_element_type=jnp.float32
    ).reshape(NSIG, 2, NFREQ, FACES_OWN)
    parts = arrived[:, OBS_ROW : OBS_ROW + 18].astype(jnp.float32)
    parts = parts.reshape(owners, 3, 3, OBS_TILE)
    observers = (parts[:, 0] + parts[:, 1]) + parts[:, 2]
    shift = jnp.asarray([CENTER_X, 0.0, 0.0], jnp.float32)
    observers = observers - shift[None, :, None]
    geom = face_geom - jnp.asarray([CENTER_X, 0.0, 0.0, 0.0], jnp.float32)[:, None]
    out = partial_pressure(face_weights(spec, geom), geom, observers)
    out = out.reshape(owners * groups, 2 * NFREQ // groups, OBS_TILE)
    got = lax.all_to_all(out, ("obs", "grp"), split_axis=0, concat_axis=0, tiled=True)
    return jnp.sum(got, axis=0)


def solution(mesh):
    return jax.shard_map(
        local,
        mesh=mesh,
        in_specs=(
            P(None, None, ("grp", "obs")),
            P(("grp", "obs")),
            P(("grp", "obs")),
            P(None, ("grp", "obs")),
            P(None, "obs"),
        ),
        out_specs=P("grp", "obs"),
        check_vma=False,
    )
```

```python
import math

import jax
import jax.numpy as jnp
import numpy as np
from jax import lax
from jax.experimental import pallas as pl
from jax.experimental.pallas import tpu as pltpu
from jax.sharding import PartitionSpec as P

SAMPLES = 256
NFREQ = 8
NSIG = 4
PATCH = 128
MAXP = 8
PER_OWN = 4
FACES_OWN = 512
CHANNELS = NSIG * 2 * NFREQ
ROWS_MSG = 80
OBS_ROW = 64
OBS_TILE = 256
CHUNK = 64
TERMS = 16
HALF = FACES_OWN // 2
HALF_CHUNKS = HALF // CHUNK
UNIT = 0.25 / math.pi
CENTER_X = 15.0

COS_COEFS = (
    0.9999992107823207,
    -19.73898035576387,
    64.92865742102978,
    -85.27162153426406,
    58.790492119980826,
    -21.071105627415147,
)
SIN_COEFS = (
    6.283184916495429,
    -41.34158923268831,
    81.59994332977428,
    -76.61447253115396,
    41.342882354135696,
    -12.471243534350362,
)


def spectral_basis():
    t = np.arange(SAMPLES, dtype=np.float64)
    m = np.arange(1, NFREQ + 1, dtype=np.float64)
    angles = 2.0 * math.pi / SAMPLES * (t[:, None] * m[None, :])
    window = (0.5 - 0.5 * np.cos(2.0 * math.pi / SAMPLES * t)) * math.sqrt(8.0 / (3.0 * SAMPLES))
    table = np.concatenate(
        [window[:, None] * np.cos(angles), -window[:, None] * np.sin(angles)], axis=1
    )
    return jnp.asarray(table.T.astype(np.float32)).astype(jnp.bfloat16)


def pack_kernel(count_ref, place_ref, basis_ref, signals_ref, obs_ref, out_ref):
    sig = pl.program_id(0)

    @pl.when(sig == 0)
    def _():
        x = obs_ref[...]
        hi = x.astype(jnp.bfloat16).astype(jnp.float32)
        rows = []
        for part in (hi, x - hi):
            for c in range(3):
                for h in range(2):
                    rows.append(part[c : c + 1, h * PATCH : (h + 1) * PATCH])
        tail = jnp.concatenate(rows + [jnp.zeros((4, PATCH), jnp.float32)], axis=0)
        out_ref[...] = jnp.zeros_like(out_ref)
        for o in range(out_ref.shape[0]):
            out_ref[o, OBS_ROW:, :] = tail.astype(jnp.bfloat16)
        row_id = lax.broadcasted_iota(jnp.int32, (16, PATCH), 0)
        for j in range(MAXP):
            place = place_ref[j]
            owner = place // PER_OWN
            part_no = (place % PER_OWN + 1).astype(jnp.float32)

            @pl.when(j < count_ref[0])
            def _():
                out_ref[owner, OBS_ROW:, :] = jnp.where(row_id < 12, tail, part_no).astype(
                    jnp.bfloat16
                )

    spec = jnp.dot(
        basis_ref[...], signals_ref[0], preferred_element_type=jnp.float32
    ).astype(jnp.bfloat16)
    row0 = pl.multiple_of(sig * 16, 16)
    for j in range(MAXP):

        @pl.when(j < count_ref[0])
        def _():
            owner = place_ref[j] // PER_OWN
            out_ref[owner, pl.ds(row0, 16), :] = spec[:, j * PATCH : (j + 1) * PATCH]


def pack(signals, patch_count, patch_place, obs_pos, owners):
    return pl.pallas_call(
        pack_kernel,
        grid=(NSIG,),
        in_specs=[
            pl.BlockSpec(memory_space=pltpu.SMEM),
            pl.BlockSpec(memory_space=pltpu.SMEM),
            pl.BlockSpec((2 * NFREQ, SAMPLES), lambda s: (0, 0)),
            pl.BlockSpec((1, SAMPLES, MAXP * PATCH), lambda s: (s, 0, 0)),
            pl.BlockSpec(obs_pos.shape, lambda s: (0, 0)),
        ],
        out_specs=pl.BlockSpec((owners, ROWS_MSG, PATCH), lambda s: (0, 0, 0)),
        out_shape=jax.ShapeDtypeStruct((owners, ROWS_MSG, PATCH), jnp.bfloat16),
        name="pack",
    )(patch_count, patch_place, spectral_basis(), signals, obs_pos)


def horner(coefs, z):
    acc = jnp.full_like(z, coefs[-1])
    for c in coefs[-2::-1]:
        acc = acc * z + c
    return acc


def face_matrices(t, f0, at, obs_ref, face_ref, g_ref):
    x = [obs_ref[t, c : c + 1, :] for c in range(3)]
    for group in range(CHUNK // 16):
        y = []
        for c in range(4):
            col = face_ref[c, f0 + group * 16 : f0 + group * 16 + 16, :]
            y.append(jnp.concatenate([col, col], axis=1))
        dx = x[0] - y[0]
        dy = x[1] - y[1]
        dz = x[2] - y[2]
        r2 = dx * dx + dy * dy + dz * dz
        inv = lax.rsqrt(r2)
        r = r2 * inv
        frac = r - jnp.round(r)
        z = frac * frac
        cos1 = horner(COS_COEFS, z)
        sin1 = horner(SIN_COEFS, z) * frac
        amp = y[3] * inv * (inv * inv)
        two_cos = cos1 + cos1
        c_old, s_old = amp, None
        c_now, s_now = amp * cos1, amp * sin1
        for m in range(NFREQ):
            if m == 1:
                c_old, c_now = c_now, two_cos * c_now - c_old
                s_old, s_now = s_now, two_cos * s_now
            elif m > 1:
                c_old, c_now = c_now, two_cos * c_now - c_old
                s_old, s_now = s_now, two_cos * s_now - s_old
            for family, v in enumerate((c_now * r, s_now * r, c_now, s_now)):
                row = family * HALF + at + group * 16
                g_ref[m, row : row + 16, :] = v.astype(jnp.bfloat16)


def half_product(m, half, w_ref, g_ref):
    return jnp.dot(
        w_ref[m, :, half * 4 * HALF : (half + 1) * 4 * HALF],
        g_ref[m],
        preferred_element_type=jnp.float32,
    )


def finish(t, m, total, obs_ref, out_ref):
    x = [obs_ref[t, c : c + 1, :] for c in range(3)]
    xx = x[0] * x[0] + x[1] * x[1] + x[2] * x[2]
    scale = 0.5 * (m + 1) / (16.0 * math.pi**2)
    for part in range(2):
        row = lambda n: total[2 * n + part : 2 * n + part + 1, :]
        value = xx * row(0) + row(1) + row(2)
        value = value + x[0] * (row(3) + row(6)) + x[1] * (row(4) + row(7)) + x[2] * row(5)
        value = value * scale
        at = part * NFREQ + m
        for h in range(2):
            line = 2 * (at % 2) + h
            out_ref[at // 2, t, line : line + 1, :] = value[:, h * PATCH : (h + 1) * PATCH]


def build_observers(arrived_ref, obs_ref):
    for t in range(arrived_ref.shape[0]):
        rows = arrived_ref[t, OBS_ROW : OBS_ROW + 16, :].astype(jnp.float32)
        pos = rows[0:6] + rows[6:12]
        for c in range(3):
            line = jnp.concatenate([pos[2 * c : 2 * c + 1], pos[2 * c + 1 : 2 * c + 2]], axis=1)
            line = (line - CENTER_X if c == 0 else line) * UNIT
            obs_ref[t, c : c + 1, :] = line


def build_faces(geom_ref, geo_ref, face_ref):
    geo_ref[0:1, :] = (geom_ref[0:1, :] - CENTER_X) * UNIT
    geo_ref[1:3, :] = geom_ref[1:3, :] * UNIT
    geo_ref[3:4, :] = geom_ref[3:4, :]
    geo_ref[4:8, :] = jnp.zeros((4, FACES_OWN), jnp.float32)
    cols = geo_ref[...].T
    for c in range(4):
        face_ref[c] = jnp.broadcast_to(cols[:, c : c + 1], (FACES_OWN, PATCH))


def build_weights(arrived_ref, geo_ref, wide_ref, w_ref):
    inv_k = 1.0 / (
        2.0
        * math.pi
        * (1 + lax.broadcasted_iota(jnp.int32, (NFREQ, PATCH), 0)).astype(jnp.float32)
    )
    for j in range(PER_OWN):
        spec = jnp.zeros((CHANNELS, PATCH), jnp.float32)
        for o in range(arrived_ref.shape[0]):
            tail = arrived_ref[o, OBS_ROW : OBS_ROW + 16, :].astype(jnp.float32)
            picked = (tail[15:16, :] == float(j + 1)).astype(jnp.float32)
            spec = spec + arrived_ref[o, 0:CHANNELS, :].astype(jnp.float32) * picked
        y = [geo_ref[c : c + 1, j * PATCH : (j + 1) * PATCH] for c in range(3)]
        yy = y[0] * y[0] + y[1] * y[1] + y[2] * y[2]
        qr, qi = spec[0:8], spec[8:16]
        lr = [spec[16 + 16 * c : 24 + 16 * c] for c in range(3)]
        li = [spec[24 + 16 * c : 32 + 16 * c] for c in range(3)]
        lyr = lr[0] * y[0] + lr[1] * y[1] + lr[2] * y[2]
        lyi = li[0] * y[0] + li[1] * y[1] + li[2] * y[2]
        zero = jnp.zeros_like(qr)

        def four(load_r, load_i, mono):
            near_r, near_i = load_r * inv_k, load_i * inv_k
            mono_r, mono_i = mono * qr, mono * qi
            return (
                (-load_i, load_r, near_r - mono_i, near_i + mono_r),
                (load_r, load_i, near_i + mono_r, mono_i - near_r),
            )

        half, at = divmod(j * PATCH, HALF)

        def put(term, family, value):
            block = ((half * 4 + family) * HALF + at) // PATCH
            wide_ref[block, pl.ds(term, NFREQ, stride=TERMS), :] = value

        square = ((zero, zero, -qi, qr), (zero, zero, qr, qi))
        base = four(-lyr, -lyi, yy)
        load = [four(lr[c], li[c], -2.0 * y[c]) for c in range(3)]
        for part in range(2):
            for family in range(4):
                put(part, family, square[part][family])
                hi = base[part][family].astype(jnp.bfloat16).astype(jnp.float32)
                put(2 + part, family, hi)
                put(4 + part, family, base[part][family] - hi)
                for c in range(3):
                    value = load[c][part][family]
                    hi = value.astype(jnp.bfloat16).astype(jnp.float32)
                    put(6 + 2 * c + part, family, hi)
                    if c < 2:
                        put(12 + 2 * c + part, family, value - hi)
    for m in range(NFREQ):
        for block in range(wide_ref.shape[0]):
            w_ref[m, :, block * PATCH : (block + 1) * PATCH] = wide_ref[
                block, m * TERMS : (m + 1) * TERMS, :
            ].astype(jnp.bfloat16)


def pressure_kernel(
    arrived_ref, geom_ref, out_ref, obs_ref, geo_ref, face_ref, wide_ref, w_ref, ga_ref, gb_ref, acc_ref
):
    tiles = arrived_ref.shape[0]
    build_observers(arrived_ref, obs_ref)
    build_faces(geom_ref, geo_ref, face_ref)
    build_weights(arrived_ref, geo_ref, wide_ref, w_ref)
    per_chunk = NFREQ // HALF_CHUNKS

    def tile(t, carry):
        before = jnp.maximum(t - 1, 0)
        for j in range(HALF_CHUNKS):
            face_matrices(t, j * CHUNK, j * CHUNK, obs_ref, face_ref, ga_ref)
            for m in range(j * per_chunk, (j + 1) * per_chunk):
                total = acc_ref[m] + half_product(m, 1, w_ref, gb_ref)
                finish(before, m, total, obs_ref, out_ref)
        for j in range(HALF_CHUNKS):
            face_matrices(t, HALF + j * CHUNK, j * CHUNK, obs_ref, face_ref, gb_ref)
            for m in range(j * per_chunk, (j + 1) * per_chunk):
                acc_ref[m] = half_product(m, 0, w_ref, ga_ref)
        return carry

    lax.fori_loop(0, tiles, tile, 0)
    for m in range(NFREQ):
        total = acc_ref[m] + half_product(m, 1, w_ref, gb_ref)
        finish(tiles - 1, m, total, obs_ref, out_ref)


def partial_pressure(arrived, geom):
    tiles = arrived.shape[0]
    return pl.pallas_call(
        pressure_kernel,
        in_specs=[pl.BlockSpec(memory_space=pltpu.VMEM)] * 2,
        out_specs=pl.BlockSpec(memory_space=pltpu.VMEM),
        out_shape=jax.ShapeDtypeStruct((NFREQ, tiles, 4, PATCH), jnp.float32),
        scratch_shapes=[
            pltpu.VMEM((tiles, 8, OBS_TILE), jnp.float32),
            pltpu.VMEM((8, FACES_OWN), jnp.float32),
            pltpu.VMEM((4, FACES_OWN, PATCH), jnp.float32),
            pltpu.VMEM((4 * FACES_OWN // PATCH, NFREQ * TERMS, PATCH), jnp.float32),
            pltpu.VMEM((NFREQ, TERMS, 4 * FACES_OWN), jnp.bfloat16),
            pltpu.VMEM((NFREQ, 4 * HALF, OBS_TILE), jnp.bfloat16),
            pltpu.VMEM((NFREQ, 4 * HALF, OBS_TILE), jnp.bfloat16),
            pltpu.VMEM((NFREQ, TERMS, OBS_TILE), jnp.float32),
        ],
        compiler_params=pltpu.CompilerParams(vmem_limit_bytes=48 * 1024 * 1024),
        name="pressure",
    )(arrived, geom)


def local(signals, patch_count, patch_place, face_geom, obs_pos):
    owners = lax.axis_size("obs")
    groups = lax.axis_size("grp")
    outgoing = pack(signals, patch_count, patch_place, obs_pos, owners)
    arrived = lax.all_to_all(outgoing, "obs", split_axis=0, concat_axis=0, tiled=True)
    out = partial_pressure(arrived, face_geom)
    out = out.reshape(groups * owners, 4, PATCH)
    got = lax.all_to_all(out, ("grp", "obs"), split_axis=0, concat_axis=0, tiled=True)
    return jnp.sum(got, axis=0).reshape(2 * NFREQ // groups, OBS_TILE)


def solution(mesh):
    return jax.shard_map(
        local,
        mesh=mesh,
        in_specs=(
            P(None, None, ("grp", "obs")),
            P(("grp", "obs")),
            P(("grp", "obs")),
            P(None, ("grp", "obs")),
            P(None, "obs"),
        ),
        out_specs=P("grp", "obs"),
        check_vma=False,
    )
```

```python
import math

import jax
import jax.numpy as jnp
import numpy as np
from jax import lax
from jax.experimental import pallas as pl
from jax.experimental.pallas import tpu as pltpu
from jax.sharding import PartitionSpec as P

SAMPLES = 256
NFREQ = 8
NSIG = 4
PATCH = 128
MAXP = 8
PER_OWN = 4
FACES_OWN = 512
CHANNELS = NSIG * 2 * NFREQ
ROWS_MSG = 80
OBS_ROW = 64
OBS_TILE = 256
TERMS = 16
CHUNK = 64
CHUNKS = FACES_OWN // CHUNK
UNIT = 0.25 / math.pi
CENTER_X = 15.0

COS_COEFS = (
    0.9999992107823207,
    -19.73898035576387,
    64.92865742102978,
    -85.27162153426406,
    58.790492119980826,
    -21.071105627415147,
)
SIN_COEFS = (
    6.283184916495429,
    -41.34158923268831,
    81.59994332977428,
    -76.61447253115396,
    41.342882354135696,
    -12.471243534350362,
)


def spectral_basis():
    t = np.arange(SAMPLES, dtype=np.float64)
    m = np.arange(1, NFREQ + 1, dtype=np.float64)
    angles = 2.0 * math.pi / SAMPLES * (t[:, None] * m[None, :])
    window = (0.5 - 0.5 * np.cos(2.0 * math.pi / SAMPLES * t)) * math.sqrt(8.0 / (3.0 * SAMPLES))
    table = np.concatenate(
        [window[:, None] * np.cos(angles), -window[:, None] * np.sin(angles)], axis=1
    )
    return jnp.asarray(table.T.astype(np.float32)).astype(jnp.bfloat16)


def pack_kernel(count_ref, place_ref, basis_ref, signals_ref, obs_ref, out_ref):
    sig = pl.program_id(0)

    @pl.when(sig == 0)
    def _():
        x = obs_ref[...]
        hi = x.astype(jnp.bfloat16).astype(jnp.float32)
        rows = []
        for part in (hi, x - hi):
            for c in range(3):
                for h in range(2):
                    rows.append(part[c : c + 1, h * PATCH : (h + 1) * PATCH])
        tail = jnp.concatenate(rows + [jnp.zeros((4, PATCH), jnp.float32)], axis=0)
        out_ref[...] = jnp.zeros_like(out_ref)
        for o in range(out_ref.shape[0]):
            out_ref[o, OBS_ROW:, :] = tail.astype(jnp.bfloat16)
        row_id = lax.broadcasted_iota(jnp.int32, (16, PATCH), 0)
        for j in range(MAXP):
            place = place_ref[j]
            owner = place // PER_OWN
            part_no = (place % PER_OWN + 1).astype(jnp.float32)

            @pl.when(j < count_ref[0])
            def _():
                out_ref[owner, OBS_ROW:, :] = jnp.where(row_id < 12, tail, part_no).astype(
                    jnp.bfloat16
                )

    spec = jnp.dot(
        basis_ref[...], signals_ref[0], preferred_element_type=jnp.float32
    ).astype(jnp.bfloat16)
    row0 = pl.multiple_of(sig * 16, 16)
    for j in range(MAXP):

        @pl.when(j < count_ref[0])
        def _():
            owner = place_ref[j] // PER_OWN
            out_ref[owner, pl.ds(row0, 16), :] = spec[:, j * PATCH : (j + 1) * PATCH]


def pack(signals, patch_count, patch_place, obs_pos, owners):
    return pl.pallas_call(
        pack_kernel,
        grid=(NSIG,),
        in_specs=[
            pl.BlockSpec(memory_space=pltpu.SMEM),
            pl.BlockSpec(memory_space=pltpu.SMEM),
            pl.BlockSpec((2 * NFREQ, SAMPLES), lambda s: (0, 0)),
            pl.BlockSpec((1, SAMPLES, MAXP * PATCH), lambda s: (s, 0, 0)),
            pl.BlockSpec(obs_pos.shape, lambda s: (0, 0)),
        ],
        out_specs=pl.BlockSpec((owners, ROWS_MSG, PATCH), lambda s: (0, 0, 0)),
        out_shape=jax.ShapeDtypeStruct((owners, ROWS_MSG, PATCH), jnp.bfloat16),
        name="pack",
    )(patch_count, patch_place, spectral_basis(), signals, obs_pos)


def horner(coefs, z):
    acc = jnp.full_like(z, coefs[-1])
    for c in coefs[-2::-1]:
        acc = acc * z + c
    return acc


def add_chunk(t, chunk, obs_ref, face_ref, w_ref, acc_ref):
    state = []
    x = [obs_ref[t, c : c + 1, :] for c in range(4)]
    for group in range(CHUNK // 16):
        rows = slice(chunk * CHUNK + group * 16, chunk * CHUNK + group * 16 + 16)
        y = []
        for c in range(5):
            col = face_ref[c, rows, :]
            y.append(jnp.concatenate([col, col], axis=1))
        r2 = (x[3] + y[3]) + x[0] * y[0] + x[1] * y[1] + x[2] * y[2]
        inv = lax.rsqrt(r2)
        r = r2 * inv
        amp = y[4] * (inv * inv)
        frac = r - jnp.round(r)
        z = frac * frac
        cos1 = horner(COS_COEFS, z)
        sin1 = horner(SIN_COEFS, z) * frac
        state.append([cos1 + cos1, inv.astype(jnp.bfloat16), amp, amp * cos1, None, amp * sin1])
    for m in range(NFREQ):
        pieces = []
        for one in state:
            two_cos, other, c_old, c_now, s_old, s_now = one
            if m == 1:
                c_old, c_now = c_now, two_cos * c_now - c_old
                s_old, s_now = s_now, two_cos * s_now
            elif m > 1:
                c_old, c_now = c_now, two_cos * c_now - c_old
                s_old, s_now = s_now, two_cos * s_now - s_old
            one[2:] = [c_old, c_now, s_old, s_now]
            c_half, s_half = c_now.astype(jnp.bfloat16), s_now.astype(jnp.bfloat16)
            pieces.append((c_half, s_half, c_half * other, s_half * other))
        g = jnp.concatenate([p[family] for family in range(4) for p in pieces], axis=0)
        part = jnp.dot(w_ref[chunk, m], g, preferred_element_type=jnp.float32)
        acc_ref[m] = part if chunk == 0 else acc_ref[m] + part


def finish(t, obs_ref, acc_ref, out_ref):
    x = [obs_ref[t, c : c + 1, :] for c in range(3)]
    xx = obs_ref[t, 3:4, :]
    for m in range(NFREQ):
        total = acc_ref[m]
        scale = 0.5 * (m + 1) / (16.0 * math.pi**2)
        for part in range(2):
            row = lambda n: total[2 * n + part : 2 * n + part + 1, :]
            value = xx * row(0) + row(1) + row(2)
            value = value + x[0] * (row(3) + row(6)) + x[1] * (row(4) + row(7)) + x[2] * row(5)
            value = value * scale
            at = part * NFREQ + m
            for h in range(2):
                line = 2 * (at % 2) + h
                out_ref[at // 2, t, line : line + 1, :] = value[:, h * PATCH : (h + 1) * PATCH]


def build_observers(arrived_ref, obs_ref):
    for t in range(arrived_ref.shape[0]):
        rows = arrived_ref[t, OBS_ROW : OBS_ROW + 16, :].astype(jnp.float32)
        pos = rows[0:6] + rows[6:12]
        for c in range(3):
            line = jnp.concatenate([pos[2 * c : 2 * c + 1], pos[2 * c + 1 : 2 * c + 2]], axis=1)
            line = (line - CENTER_X if c == 0 else line) * UNIT
            obs_ref[t, c : c + 1, :] = line
        x = [obs_ref[t, c : c + 1, :] for c in range(3)]
        obs_ref[t, 3:4, :] = x[0] * x[0] + x[1] * x[1] + x[2] * x[2]


def build_faces(geom_ref, geo_ref, face_ref):
    geo_ref[0:1, :] = (geom_ref[0:1, :] - CENTER_X) * UNIT
    geo_ref[1:3, :] = geom_ref[1:3, :] * UNIT
    y = [geo_ref[c : c + 1, :] for c in range(3)]
    for c in range(3):
        geo_ref[4 + c : 5 + c, :] = -2.0 * y[c]
    geo_ref[3:4, :] = y[0] * y[0] + y[1] * y[1] + y[2] * y[2]
    geo_ref[7:8, :] = geom_ref[3:4, :]
    cols = geo_ref[...].T
    for c, row in enumerate((4, 5, 6, 3, 7)):
        face_ref[c] = jnp.broadcast_to(cols[:, row : row + 1], (FACES_OWN, PATCH))


def build_weights(arrived_ref, geo_ref, wide_ref, w_ref):
    inv_k = 1.0 / (
        2.0
        * math.pi
        * (1 + lax.broadcasted_iota(jnp.int32, (NFREQ, PATCH), 0)).astype(jnp.float32)
    )
    left = lax.broadcasted_iota(jnp.int32, (NFREQ, PATCH), 1) < CHUNK
    for j in range(PER_OWN):
        spec = jnp.zeros((CHANNELS, PATCH), jnp.float32)
        for o in range(arrived_ref.shape[0]):
            tail = arrived_ref[o, OBS_ROW : OBS_ROW + 16, :].astype(jnp.float32)
            picked = (tail[15:16, :] == float(j + 1)).astype(jnp.float32)
            spec = spec + arrived_ref[o, 0:CHANNELS, :].astype(jnp.float32) * picked
        y = [geo_ref[c : c + 1, j * PATCH : (j + 1) * PATCH] for c in range(3)]
        yy = geo_ref[3:4, j * PATCH : (j + 1) * PATCH]
        qr, qi = spec[0:8], spec[8:16]
        lr = [spec[16 + 16 * c : 24 + 16 * c] for c in range(3)]
        li = [spec[24 + 16 * c : 32 + 16 * c] for c in range(3)]
        lyr = lr[0] * y[0] + lr[1] * y[1] + lr[2] * y[2]
        lyi = li[0] * y[0] + li[1] * y[1] + li[2] * y[2]
        zero = jnp.zeros_like(qr)

        def four(load_r, load_i, mono):
            near_r, near_i = load_r * inv_k, load_i * inv_k
            mono_r, mono_i = mono * qr, mono * qi
            return (
                (-load_i, load_r, near_r - mono_i, near_i + mono_r),
                (load_r, load_i, near_i + mono_r, mono_i - near_r),
            )

        def put(term, values):
            for pair in range(2):
                a, b = values[2 * pair], values[2 * pair + 1]
                first = jnp.where(left, a, pltpu.roll(b, CHUNK, axis=1))
                second = jnp.where(left, pltpu.roll(a, CHUNK, axis=1), b)
                rows = pl.ds(term, NFREQ, stride=TERMS)
                wide_ref[4 * j + pair, rows, :] = first
                wide_ref[4 * j + 2 + pair, rows, :] = second

        square = ((zero, zero, -qi, qr), (zero, zero, qr, qi))
        base = four(-lyr, -lyi, yy)
        load = [four(lr[c], li[c], -2.0 * y[c]) for c in range(3)]
        def split(values):
            hi = [v.astype(jnp.bfloat16).astype(jnp.float32) for v in values]
            return hi, [v - h for v, h in zip(values, hi)]

        for part in range(2):
            put(part, square[part])
            hi, low = split(base[part])
            put(2 + part, hi)
            put(4 + part, low)
            for c in range(3):
                hi, low = split(load[c][part])
                put(6 + 2 * c + part, hi)
                if c < 2:
                    put(12 + 2 * c + part, low)
    for chunk in range(CHUNKS):
        for m in range(NFREQ):
            for side in range(2):
                w_ref[chunk, m, :, side * PATCH : (side + 1) * PATCH] = wide_ref[
                    2 * chunk + side, m * TERMS : (m + 1) * TERMS, :
                ].astype(jnp.bfloat16)


def pressure_kernel(
    arrived_ref, geom_ref, out_ref, obs_ref, geo_ref, face_ref, wide_ref, w_ref, acc_ref
):
    tiles = arrived_ref.shape[0]
    build_observers(arrived_ref, obs_ref)
    build_faces(geom_ref, geo_ref, face_ref)
    build_weights(arrived_ref, geo_ref, wide_ref, w_ref)

    def tile(t, carry):
        finish(jnp.maximum(t - 1, 0), obs_ref, acc_ref, out_ref)
        for chunk in range(CHUNKS):
            add_chunk(t, chunk, obs_ref, face_ref, w_ref, acc_ref)
        return carry

    def pair(i, carry):
        return tile(2 * i + 1, tile(2 * i, carry))

    lax.fori_loop(0, tiles // 2, pair, 0)
    finish(tiles - 1, obs_ref, acc_ref, out_ref)


def partial_pressure(arrived, geom):
    tiles = arrived.shape[0]
    return pl.pallas_call(
        pressure_kernel,
        in_specs=[pl.BlockSpec(memory_space=pltpu.VMEM)] * 2,
        out_specs=pl.BlockSpec(memory_space=pltpu.VMEM),
        out_shape=jax.ShapeDtypeStruct((NFREQ, tiles, 4, PATCH), jnp.float32),
        scratch_shapes=[
            pltpu.VMEM((tiles, 8, OBS_TILE), jnp.float32),
            pltpu.VMEM((8, FACES_OWN), jnp.float32),
            pltpu.VMEM((5, FACES_OWN, PATCH), jnp.float32),
            pltpu.VMEM((4 * FACES_OWN // PATCH, NFREQ * TERMS, PATCH), jnp.float32),
            pltpu.VMEM((CHUNKS, NFREQ, TERMS, 4 * CHUNK), jnp.bfloat16),
            pltpu.VMEM((NFREQ, TERMS, OBS_TILE), jnp.float32),
        ],
        compiler_params=pltpu.CompilerParams(vmem_limit_bytes=48 * 1024 * 1024),
        name="pressure",
    )(arrived, geom)


def local(signals, patch_count, patch_place, face_geom, obs_pos):
    owners = lax.axis_size("obs")
    groups = lax.axis_size("grp")
    outgoing = pack(signals, patch_count, patch_place, obs_pos, owners)
    arrived = lax.all_to_all(outgoing, "obs", split_axis=0, concat_axis=0, tiled=True)
    out = partial_pressure(arrived, face_geom)
    out = out.reshape(groups * owners, 4, PATCH)
    got = lax.all_to_all(out, ("grp", "obs"), split_axis=0, concat_axis=0, tiled=True)
    return jnp.sum(got, axis=0).reshape(2 * NFREQ // groups, OBS_TILE)


def solution(mesh):
    return jax.shard_map(
        local,
        mesh=mesh,
        in_specs=(
            P(None, None, ("grp", "obs")),
            P(("grp", "obs")),
            P(("grp", "obs")),
            P(None, ("grp", "obs")),
            P(None, "obs"),
        ),
        out_specs=P("grp", "obs"),
        check_vma=False,
    )
```

```python
import math

import jax
import jax.numpy as jnp
import numpy as np
from jax import lax
from jax.experimental import pallas as pl
from jax.experimental.pallas import tpu as pltpu
from jax.sharding import PartitionSpec as P

SAMPLES = 256
NFREQ = 8
NSIG = 4
PATCH = 128
MAXP = 8
PER_OWN = 4
FACES_OWN = 512
CHANNELS = NSIG * 2 * NFREQ
ROWS_MSG = 80
OBS_ROW = 64
OBS_TILE = 256
TERMS = 16
CHUNK = 64
CHUNKS = FACES_OWN // CHUNK
UNIT = 0.25 / math.pi
CENTER_X = 15.0

COS_COEFS = (
    0.9999992107823207,
    -19.73898035576387,
    64.92865742102978,
    -85.27162153426406,
    58.790492119980826,
    -21.071105627415147,
)
SIN_COEFS = (
    6.283184916495429,
    -41.34158923268831,
    81.59994332977428,
    -76.61447253115396,
    41.342882354135696,
    -12.471243534350362,
)


def spectral_basis():
    t = np.arange(SAMPLES, dtype=np.float64)
    m = np.arange(1, NFREQ + 1, dtype=np.float64)
    angles = 2.0 * math.pi / SAMPLES * (t[:, None] * m[None, :])
    window = (0.5 - 0.5 * np.cos(2.0 * math.pi / SAMPLES * t)) * math.sqrt(8.0 / (3.0 * SAMPLES))
    table = np.concatenate(
        [window[:, None] * np.cos(angles), -window[:, None] * np.sin(angles)], axis=1
    )
    return jnp.asarray(table.T.astype(np.float32)).astype(jnp.bfloat16)


def pack_kernel(
    count_hbm, place_hbm, basis_ref, signals_hbm, obs_ref, out_ref, count_ref, place_ref, rows_ref, sems
):
    small = [
        pltpu.make_async_copy(count_hbm, count_ref, sems.at[NSIG]),
        pltpu.make_async_copy(place_hbm, place_ref, sems.at[NSIG + 1]),
    ]
    large = [
        pltpu.make_async_copy(signals_hbm.at[s], rows_ref.at[s], sems.at[s]) for s in range(NSIG)
    ]
    for copy in small + large:
        copy.start()
    x = obs_ref[...]
    hi = x.astype(jnp.bfloat16).astype(jnp.float32)
    rows = []
    for part in (hi, x - hi):
        for c in range(3):
            for h in range(2):
                rows.append(part[c : c + 1, h * PATCH : (h + 1) * PATCH])
    tail = jnp.concatenate(rows + [jnp.zeros((4, PATCH), jnp.float32)], axis=0)
    for o in range(out_ref.shape[0]):
        out_ref[o, 0:CHANNELS, :] = jnp.zeros((CHANNELS, PATCH), jnp.bfloat16)
        out_ref[o, OBS_ROW:, :] = tail.astype(jnp.bfloat16)
    row_id = lax.broadcasted_iota(jnp.int32, (16, PATCH), 0)
    for copy in small:
        copy.wait()
    count = count_ref[0, 0]
    for j in range(MAXP):
        place = place_ref[j]
        part_no = (place % PER_OWN + 1).astype(jnp.float32)

        @pl.when(j < count)
        def _():
            out_ref[place // PER_OWN, OBS_ROW:, :] = jnp.where(row_id < 12, tail, part_no).astype(
                jnp.bfloat16
            )

    for s in range(NSIG):
        large[s].wait()
        spec = jnp.dot(
            basis_ref[...], rows_ref[s], preferred_element_type=jnp.float32
        ).astype(jnp.bfloat16)
        for j in range(MAXP):

            @pl.when(j < count)
            def _():
                owner = place_ref[j] // PER_OWN
                out_ref[owner, s * 16 : s * 16 + 16, :] = spec[:, j * PATCH : (j + 1) * PATCH]


def pack(signals, patch_count, patch_place, obs_pos, owners):
    hbm = pl.BlockSpec(memory_space=pltpu.MemorySpace.HBM)
    vmem = pl.BlockSpec(memory_space=pltpu.VMEM)
    return pl.pallas_call(
        pack_kernel,
        in_specs=[hbm, hbm, vmem, hbm, vmem],
        out_specs=vmem,
        out_shape=jax.ShapeDtypeStruct((owners, ROWS_MSG, PATCH), jnp.bfloat16),
        scratch_shapes=[
            pltpu.SMEM((1, 1), jnp.int32),
            pltpu.SMEM((MAXP,), jnp.int32),
            pltpu.VMEM(signals.shape, signals.dtype),
            pltpu.SemaphoreType.DMA((NSIG + 2,)),
        ],
        compiler_params=pltpu.CompilerParams(vmem_limit_bytes=67000000),
        name="pack",
    )(patch_count.reshape(1, 1), patch_place, spectral_basis(), signals, obs_pos)


def horner(coefs, z):
    acc = jnp.full_like(z, coefs[-1])
    for c in coefs[-2::-1]:
        acc = acc * z + c
    return acc


def add_chunk(t, chunk, obs_ref, face_ref, w_ref, acc_ref):
    state = []
    x = [obs_ref[t, c : c + 1, :] for c in range(4)]
    for group in range(CHUNK // 16):
        rows = slice(chunk * CHUNK + group * 16, chunk * CHUNK + group * 16 + 16)
        y = []
        for c in range(5):
            col = face_ref[c, rows, :]
            y.append(jnp.concatenate([col, col], axis=1))
        r2 = (x[3] + y[3]) + x[0] * y[0] + x[1] * y[1] + x[2] * y[2]
        inv = lax.rsqrt(r2)
        r = r2 * inv
        amp = y[4] * (inv * inv)
        frac = r - jnp.round(r)
        z = frac * frac
        cos1 = horner(COS_COEFS, z)
        sin1 = horner(SIN_COEFS, z) * frac
        state.append([cos1 + cos1, inv.astype(jnp.bfloat16), amp, amp * cos1, None, amp * sin1])
    for m in range(NFREQ):
        pieces = []
        for one in state:
            two_cos, other, c_old, c_now, s_old, s_now = one
            if m == 1:
                c_old, c_now = c_now, two_cos * c_now - c_old
                s_old, s_now = s_now, two_cos * s_now
            elif m > 1:
                c_old, c_now = c_now, two_cos * c_now - c_old
                s_old, s_now = s_now, two_cos * s_now - s_old
            one[2:] = [c_old, c_now, s_old, s_now]
            c_half, s_half = c_now.astype(jnp.bfloat16), s_now.astype(jnp.bfloat16)
            pieces.append((c_half, s_half, c_half * other, s_half * other))
        g = jnp.concatenate([p[family] for family in range(4) for p in pieces], axis=0)
        part = jnp.dot(w_ref[chunk, m], g, preferred_element_type=jnp.float32)
        acc_ref[m] = part if chunk == 0 else acc_ref[m] + part


def finish(t, obs_ref, acc_ref, out_ref):
    x = [obs_ref[t, c : c + 1, :] for c in range(3)]
    xx = obs_ref[t, 3:4, :]
    for pair in range(NFREQ // 2):
        lines = ([], [])
        for m in (2 * pair, 2 * pair + 1):
            total = acc_ref[m]
            scale = 0.5 * (m + 1) / (16.0 * math.pi**2)
            for part in range(2):
                row = lambda n: total[2 * n + part : 2 * n + part + 1, :]
                value = xx * row(0) + row(1) + row(2)
                value = value + x[0] * (row(3) + row(6)) + x[1] * (row(4) + row(7)) + x[2] * row(5)
                value = value * scale
                lines[part].extend([value[:, 0:PATCH], value[:, PATCH:]])
        for part in range(2):
            block = jnp.concatenate(lines[part], axis=0)
            out_ref[part * (NFREQ // 2) + pair, t] = block.astype(out_ref.dtype)


def build_observers(arrived_ref, obs_ref):
    for t in range(arrived_ref.shape[0]):
        rows = arrived_ref[t, OBS_ROW : OBS_ROW + 16, :].astype(jnp.float32)
        pos = rows[0:6] + rows[6:12]
        for c in range(3):
            line = jnp.concatenate([pos[2 * c : 2 * c + 1], pos[2 * c + 1 : 2 * c + 2]], axis=1)
            line = (line - CENTER_X if c == 0 else line) * UNIT
            obs_ref[t, c : c + 1, :] = line
        x = [obs_ref[t, c : c + 1, :] for c in range(3)]
        obs_ref[t, 3:4, :] = x[0] * x[0] + x[1] * x[1] + x[2] * x[2]


def build_faces(geom_ref, geo_ref, face_ref):
    geo_ref[0:1, :] = (geom_ref[0:1, :] - CENTER_X) * UNIT
    geo_ref[1:3, :] = geom_ref[1:3, :] * UNIT
    y = [geo_ref[c : c + 1, :] for c in range(3)]
    for c in range(3):
        geo_ref[4 + c : 5 + c, :] = -2.0 * y[c]
    geo_ref[3:4, :] = y[0] * y[0] + y[1] * y[1] + y[2] * y[2]
    geo_ref[7:8, :] = geom_ref[3:4, :]
    cols = geo_ref[...].T
    for c, row in enumerate((4, 5, 6, 3, 7)):
        face_ref[c] = jnp.broadcast_to(cols[:, row : row + 1], (FACES_OWN, PATCH))


def build_weights(arrived_ref, geo_ref, wide_ref, w_ref):
    inv_k = 1.0 / (
        2.0
        * math.pi
        * (1 + lax.broadcasted_iota(jnp.int32, (NFREQ, PATCH), 0)).astype(jnp.float32)
    )
    left = lax.broadcasted_iota(jnp.int32, (NFREQ, PATCH), 1) < CHUNK
    for j in range(PER_OWN):
        spec = jnp.zeros((CHANNELS, PATCH), jnp.float32)
        for o in range(arrived_ref.shape[0]):
            tail = arrived_ref[o, OBS_ROW : OBS_ROW + 16, :].astype(jnp.float32)
            picked = (tail[15:16, :] == float(j + 1)).astype(jnp.float32)
            spec = spec + arrived_ref[o, 0:CHANNELS, :].astype(jnp.float32) * picked
        y = [geo_ref[c : c + 1, j * PATCH : (j + 1) * PATCH] for c in range(3)]
        yy = geo_ref[3:4, j * PATCH : (j + 1) * PATCH]
        qr, qi = spec[0:8], spec[8:16]
        lr = [spec[16 + 16 * c : 24 + 16 * c] for c in range(3)]
        li = [spec[24 + 16 * c : 32 + 16 * c] for c in range(3)]
        lyr = lr[0] * y[0] + lr[1] * y[1] + lr[2] * y[2]
        lyi = li[0] * y[0] + li[1] * y[1] + li[2] * y[2]
        zero = jnp.zeros_like(qr)

        def four(load_r, load_i, mono):
            near_r, near_i = load_r * inv_k, load_i * inv_k
            mono_r, mono_i = mono * qr, mono * qi
            return (
                (-load_i, load_r, near_r - mono_i, near_i + mono_r),
                (load_r, load_i, near_i + mono_r, mono_i - near_r),
            )

        def put(term, values):
            for pair in range(2):
                a, b = values[2 * pair], values[2 * pair + 1]
                first = jnp.where(left, a, pltpu.roll(b, CHUNK, axis=1))
                second = jnp.where(left, pltpu.roll(a, CHUNK, axis=1), b)
                rows = pl.ds(term, NFREQ, stride=TERMS)
                wide_ref[4 * j + pair, rows, :] = first
                wide_ref[4 * j + 2 + pair, rows, :] = second

        square = ((zero, zero, -qi, qr), (zero, zero, qr, qi))
        base = four(-lyr, -lyi, yy)
        load = [four(lr[c], li[c], -2.0 * y[c]) for c in range(3)]
        def split(values):
            hi = [v.astype(jnp.bfloat16).astype(jnp.float32) for v in values]
            return hi, [v - h for v, h in zip(values, hi)]

        for part in range(2):
            put(part, square[part])
            hi, low = split(base[part])
            put(2 + part, hi)
            put(4 + part, low)
            for c in range(3):
                hi, low = split(load[c][part])
                put(6 + 2 * c + part, hi)
                if c < 2:
                    put(12 + 2 * c + part, low)
    for chunk in range(CHUNKS):
        for m in range(NFREQ):
            for side in range(2):
                w_ref[chunk, m, :, side * PATCH : (side + 1) * PATCH] = wide_ref[
                    2 * chunk + side, m * TERMS : (m + 1) * TERMS, :
                ].astype(jnp.bfloat16)


def pressure_kernel(
    arrived_ref, geom_ref, out_ref, obs_ref, geo_ref, face_ref, wide_ref, w_ref, acc_ref
):
    tiles = arrived_ref.shape[0]
    build_observers(arrived_ref, obs_ref)
    build_faces(geom_ref, geo_ref, face_ref)
    build_weights(arrived_ref, geo_ref, wide_ref, w_ref)

    def tile(t, carry):
        finish(jnp.maximum(t - 1, 0), obs_ref, acc_ref, out_ref)
        for chunk in range(CHUNKS):
            add_chunk(t, chunk, obs_ref, face_ref, w_ref, acc_ref)
        return carry

    def pair(i, carry):
        return tile(2 * i + 1, tile(2 * i, carry))

    lax.fori_loop(0, tiles // 2, pair, 0)
    finish(tiles - 1, obs_ref, acc_ref, out_ref)


def partial_pressure(arrived, geom):
    tiles = arrived.shape[0]
    return pl.pallas_call(
        pressure_kernel,
        in_specs=[pl.BlockSpec(memory_space=pltpu.VMEM)] * 2,
        out_specs=pl.BlockSpec(memory_space=pltpu.VMEM),
        out_shape=jax.ShapeDtypeStruct((NFREQ, tiles, 4, PATCH), jnp.bfloat16),
        scratch_shapes=[
            pltpu.VMEM((tiles, 8, OBS_TILE), jnp.float32),
            pltpu.VMEM((8, FACES_OWN), jnp.float32),
            pltpu.VMEM((5, FACES_OWN, PATCH), jnp.float32),
            pltpu.VMEM((4 * FACES_OWN // PATCH, NFREQ * TERMS, PATCH), jnp.float32),
            pltpu.VMEM((CHUNKS, NFREQ, TERMS, 4 * CHUNK), jnp.bfloat16),
            pltpu.VMEM((NFREQ, TERMS, OBS_TILE), jnp.float32),
        ],
        compiler_params=pltpu.CompilerParams(vmem_limit_bytes=48 * 1024 * 1024),
        name="pressure",
    )(arrived, geom)


def local(signals, patch_count, patch_place, face_geom, obs_pos):
    owners = lax.axis_size("obs")
    groups = lax.axis_size("grp")
    outgoing = pack(signals, patch_count, patch_place, obs_pos, owners)
    arrived = lax.all_to_all(outgoing, "obs", split_axis=0, concat_axis=0, tiled=True)
    out = partial_pressure(arrived, face_geom)
    out = out.reshape(groups * owners, 4, PATCH)
    got = lax.all_to_all(out, ("grp", "obs"), split_axis=0, concat_axis=0, tiled=True)
    return jnp.sum(got.astype(jnp.float32), axis=0).reshape(2 * NFREQ // groups, OBS_TILE)


def solution(mesh):
    return jax.shard_map(
        local,
        mesh=mesh,
        in_specs=(
            P(None, None, ("grp", "obs")),
            P(("grp", "obs")),
            P(("grp", "obs")),
            P(None, ("grp", "obs")),
            P(None, "obs"),
        ),
        out_specs=P("grp", "obs"),
        check_vma=False,
    )
```

```python
import math

import jax
import jax.numpy as jnp
import numpy as np
from jax import lax
from jax.experimental import pallas as pl
from jax.experimental.pallas import tpu as pltpu
from jax.sharding import PartitionSpec as P

SAMPLES = 256
NFREQ = 8
NSIG = 4
PATCH = 128
MAXP = 8
PER_OWN = 4
FACES_OWN = 512
CHANNELS = NSIG * 2 * NFREQ
ROWS_MSG = 80
OBS_ROW = 64
OBS_TILE = 256
TERMS = 16
CHUNK = 64
CHUNKS = FACES_OWN // CHUNK
UNIT = 0.25 / math.pi
CENTER_X = 15.0

COS_COEFS = (
    0.9999992107823207,
    -19.73898035576387,
    64.92865742102978,
    -85.27162153426406,
    58.790492119980826,
    -21.071105627415147,
)
SIN_COEFS = (
    6.283184916495429,
    -41.34158923268831,
    81.59994332977428,
    -76.61447253115396,
    41.342882354135696,
    -12.471243534350362,
)


def spectral_basis():
    t = np.arange(SAMPLES, dtype=np.float64)
    m = np.arange(1, NFREQ + 1, dtype=np.float64)
    angles = 2.0 * math.pi / SAMPLES * (t[:, None] * m[None, :])
    window = (0.5 - 0.5 * np.cos(2.0 * math.pi / SAMPLES * t)) * math.sqrt(8.0 / (3.0 * SAMPLES))
    table = np.concatenate(
        [window[:, None] * np.cos(angles), -window[:, None] * np.sin(angles)], axis=1
    )
    return jnp.asarray(table.T.astype(np.float32)).astype(jnp.bfloat16)


def pack_kernel(
    count_hbm,
    place_hbm,
    basis_hbm,
    signals_hbm,
    obs_hbm,
    out_hbm,
    count_ref,
    place_ref,
    basis_ref,
    rows_ref,
    obs_ref,
    out_ref,
    sems,
    out_sems,
):
    reads = [
        pltpu.make_async_copy(src, dst, sems.at[n])
        for n, (src, dst) in enumerate(
            [
                (obs_hbm, obs_ref),
                (count_hbm, count_ref),
                (place_hbm, place_ref),
                (basis_hbm, basis_ref),
            ]
            + [(signals_hbm.at[s], rows_ref.at[s]) for s in range(NSIG)]
        )
    ]
    writes = []
    for n in range(NSIG + 1):
        rows = slice(n * 16, n * 16 + 16)
        writes.append(
            pltpu.make_async_copy(out_ref.at[:, rows, :], out_hbm.at[:, rows, :], out_sems.at[n])
        )
    for copy in reads:
        copy.start()
    for o in range(out_ref.shape[0]):
        out_ref[o, 0:CHANNELS, :] = jnp.zeros((CHANNELS, PATCH), jnp.bfloat16)
    reads[0].wait()
    x = obs_ref[...]
    hi = x.astype(jnp.bfloat16).astype(jnp.float32)
    rows = []
    for part in (hi, x - hi):
        for c in range(3):
            for h in range(2):
                rows.append(part[c : c + 1, h * PATCH : (h + 1) * PATCH])
    tail = jnp.concatenate(rows + [jnp.zeros((4, PATCH), jnp.float32)], axis=0)
    for o in range(out_ref.shape[0]):
        out_ref[o, OBS_ROW:, :] = tail.astype(jnp.bfloat16)
    row_id = lax.broadcasted_iota(jnp.int32, (16, PATCH), 0)
    reads[1].wait()
    reads[2].wait()
    count = count_ref[0, 0]
    for j in range(MAXP):
        place = place_ref[j]
        part_no = (place % PER_OWN + 1).astype(jnp.float32)

        @pl.when(j < count)
        def _():
            out_ref[place // PER_OWN, OBS_ROW:, :] = jnp.where(row_id < 12, tail, part_no).astype(
                jnp.bfloat16
            )

    writes[NSIG].start()
    reads[3].wait()
    for s in range(NSIG):
        reads[4 + s].wait()
        spec = jnp.dot(
            basis_ref[...], rows_ref[s], preferred_element_type=jnp.float32
        ).astype(jnp.bfloat16)
        for j in range(MAXP):

            @pl.when(j < count)
            def _():
                owner = place_ref[j] // PER_OWN
                out_ref[owner, s * 16 : s * 16 + 16, :] = spec[:, j * PATCH : (j + 1) * PATCH]

        writes[s].start()
    for copy in writes:
        copy.wait()


def pack(signals, patch_count, patch_place, obs_pos, owners):
    hbm = pl.BlockSpec(memory_space=pltpu.MemorySpace.HBM)
    shape = (owners, ROWS_MSG, PATCH)
    return pl.pallas_call(
        pack_kernel,
        in_specs=[hbm] * 5,
        out_specs=hbm,
        out_shape=jax.ShapeDtypeStruct(shape, jnp.bfloat16),
        scratch_shapes=[
            pltpu.SMEM((1, 1), jnp.int32),
            pltpu.SMEM((MAXP,), jnp.int32),
            pltpu.VMEM((2 * NFREQ, SAMPLES), jnp.bfloat16),
            pltpu.VMEM(signals.shape, signals.dtype),
            pltpu.VMEM(obs_pos.shape, obs_pos.dtype),
            pltpu.VMEM(shape, jnp.bfloat16),
            pltpu.SemaphoreType.DMA((NSIG + 4,)),
            pltpu.SemaphoreType.DMA((NSIG + 1,)),
        ],
        compiler_params=pltpu.CompilerParams(vmem_limit_bytes=67000000),
        name="pack",
    )(patch_count.reshape(1, 1), patch_place, spectral_basis(), signals, obs_pos)


def horner(coefs, z):
    acc = jnp.full_like(z, coefs[-1])
    for c in coefs[-2::-1]:
        acc = acc * z + c
    return acc


def add_chunk(t, chunk, obs_ref, face_ref, w_ref, acc_ref):
    state = []
    x = [obs_ref[t, c : c + 1, :] for c in range(4)]
    for group in range(CHUNK // 16):
        rows = slice(chunk * CHUNK + group * 16, chunk * CHUNK + group * 16 + 16)
        y = []
        for c in range(5):
            col = face_ref[c, rows, :]
            y.append(jnp.concatenate([col, col], axis=1))
        r2 = (x[3] + y[3]) + x[0] * y[0] + x[1] * y[1] + x[2] * y[2]
        inv = lax.rsqrt(r2)
        r = r2 * inv
        amp = y[4] * (inv * inv)
        frac = r - jnp.round(r)
        z = frac * frac
        cos1 = horner(COS_COEFS, z)
        sin1 = horner(SIN_COEFS, z) * frac
        state.append([cos1 + cos1, inv.astype(jnp.bfloat16), amp, amp * cos1, None, amp * sin1])
    for m in range(NFREQ):
        pieces = []
        for one in state:
            two_cos, other, c_old, c_now, s_old, s_now = one
            if m == 1:
                c_old, c_now = c_now, two_cos * c_now - c_old
                s_old, s_now = s_now, two_cos * s_now
            elif m > 1:
                c_old, c_now = c_now, two_cos * c_now - c_old
                s_old, s_now = s_now, two_cos * s_now - s_old
            one[2:] = [c_old, c_now, s_old, s_now]
            c_half, s_half = c_now.astype(jnp.bfloat16), s_now.astype(jnp.bfloat16)
            pieces.append((c_half, s_half, c_half * other, s_half * other))
        g = jnp.concatenate([p[family] for family in range(4) for p in pieces], axis=0)
        part = jnp.dot(w_ref[chunk, m], g, preferred_element_type=jnp.float32)
        acc_ref[m] = part if chunk == 0 else acc_ref[m] + part


def finish(t, coef_ref, accs, out_ref):
    coef = coef_ref[t]
    for pair in range(NFREQ // 2):
        lines = ([], [])
        for m in (2 * pair, 2 * pair + 1):
            terms = accs[m] * coef
            value = terms[0:8] + terms[8:16]
            value = value + pltpu.roll(value, 4, axis=0)
            value = value + pltpu.roll(value, 2, axis=0)
            value = value * (0.5 * (m + 1) / (16.0 * math.pi**2))
            for part in range(2):
                row = value[part : part + 1]
                lines[part].extend([row[:, 0:PATCH], row[:, PATCH:]])
        for part in range(2):
            block = jnp.concatenate(lines[part], axis=0)
            out_ref[part * (NFREQ // 2) + pair, t] = block.astype(out_ref.dtype)


def build_observers(arrived_ref, obs_ref, coef_ref):
    for t in range(arrived_ref.shape[0]):
        rows = arrived_ref[t, OBS_ROW : OBS_ROW + 16, :].astype(jnp.float32)
        pos = rows[0:6] + rows[6:12]
        for c in range(3):
            line = jnp.concatenate([pos[2 * c : 2 * c + 1], pos[2 * c + 1 : 2 * c + 2]], axis=1)
            line = (line - CENTER_X if c == 0 else line) * UNIT
            obs_ref[t, c : c + 1, :] = line
        x = [obs_ref[t, c : c + 1, :] for c in range(3)]
        xx = x[0] * x[0] + x[1] * x[1] + x[2] * x[2]
        obs_ref[t, 3:4, :] = xx
        one = jnp.ones_like(xx)
        for n, row in enumerate((xx, one, one, x[0], x[1], x[2], x[0], x[1])):
            coef_ref[t, 2 * n : 2 * n + 2, :] = jnp.broadcast_to(row, (2, OBS_TILE))


def build_faces(geom_ref, geo_ref, face_ref):
    geo_ref[0:1, :] = (geom_ref[0:1, :] - CENTER_X) * UNIT
    geo_ref[1:3, :] = geom_ref[1:3, :] * UNIT
    y = [geo_ref[c : c + 1, :] for c in range(3)]
    for c in range(3):
        geo_ref[4 + c : 5 + c, :] = -2.0 * y[c]
    geo_ref[3:4, :] = y[0] * y[0] + y[1] * y[1] + y[2] * y[2]
    geo_ref[7:8, :] = geom_ref[3:4, :]
    cols = geo_ref[...].T
    for c, row in enumerate((4, 5, 6, 3, 7)):
        face_ref[c] = jnp.broadcast_to(cols[:, row : row + 1], (FACES_OWN, PATCH))


def build_weights(arrived_ref, geo_ref, wide_ref, w_ref):
    inv_k = 1.0 / (
        2.0
        * math.pi
        * (1 + lax.broadcasted_iota(jnp.int32, (NFREQ, PATCH), 0)).astype(jnp.float32)
    )
    left = lax.broadcasted_iota(jnp.int32, (NFREQ, PATCH), 1) < CHUNK
    for j in range(PER_OWN):
        spec = jnp.zeros((CHANNELS, PATCH), jnp.float32)
        for o in range(arrived_ref.shape[0]):
            tail = arrived_ref[o, OBS_ROW : OBS_ROW + 16, :].astype(jnp.float32)
            picked = (tail[15:16, :] == float(j + 1)).astype(jnp.float32)
            spec = spec + arrived_ref[o, 0:CHANNELS, :].astype(jnp.float32) * picked
        y = [geo_ref[c : c + 1, j * PATCH : (j + 1) * PATCH] for c in range(3)]
        yy = geo_ref[3:4, j * PATCH : (j + 1) * PATCH]
        qr, qi = spec[0:8], spec[8:16]
        lr = [spec[16 + 16 * c : 24 + 16 * c] for c in range(3)]
        li = [spec[24 + 16 * c : 32 + 16 * c] for c in range(3)]
        lyr = lr[0] * y[0] + lr[1] * y[1] + lr[2] * y[2]
        lyi = li[0] * y[0] + li[1] * y[1] + li[2] * y[2]
        zero = jnp.zeros_like(qr)

        def four(load_r, load_i, mono):
            near_r, near_i = load_r * inv_k, load_i * inv_k
            mono_r, mono_i = mono * qr, mono * qi
            return (
                (-load_i, load_r, near_r - mono_i, near_i + mono_r),
                (load_r, load_i, near_i + mono_r, mono_i - near_r),
            )

        def put(term, values):
            for pair in range(2):
                a, b = values[2 * pair], values[2 * pair + 1]
                first = jnp.where(left, a, pltpu.roll(b, CHUNK, axis=1))
                second = jnp.where(left, pltpu.roll(a, CHUNK, axis=1), b)
                rows = pl.ds(term, NFREQ, stride=TERMS)
                wide_ref[4 * j + pair, rows, :] = first
                wide_ref[4 * j + 2 + pair, rows, :] = second

        square = ((zero, zero, -qi, qr), (zero, zero, qr, qi))
        base = four(-lyr, -lyi, yy)
        load = [four(lr[c], li[c], -2.0 * y[c]) for c in range(3)]
        def split(values):
            hi = [v.astype(jnp.bfloat16).astype(jnp.float32) for v in values]
            return hi, [v - h for v, h in zip(values, hi)]

        for part in range(2):
            put(part, square[part])
            hi, low = split(base[part])
            put(2 + part, hi)
            put(4 + part, low)
            for c in range(3):
                hi, low = split(load[c][part])
                put(6 + 2 * c + part, hi)
                if c < 2:
                    put(12 + 2 * c + part, low)
    for chunk in range(CHUNKS):
        for m in range(NFREQ):
            for side in range(2):
                w_ref[chunk, m, :, side * PATCH : (side + 1) * PATCH] = wide_ref[
                    2 * chunk + side, m * TERMS : (m + 1) * TERMS, :
                ].astype(jnp.bfloat16)


def pressure_kernel(
    arrived_ref, geom_ref, out_ref, obs_ref, coef_ref, geo_ref, face_ref, wide_ref, w_ref, acc_ref
):
    tiles = arrived_ref.shape[0]
    build_observers(arrived_ref, obs_ref, coef_ref)
    build_faces(geom_ref, geo_ref, face_ref)
    build_weights(arrived_ref, geo_ref, wide_ref, w_ref)

    def tile(t, carry):
        finish(jnp.maximum(t - 1, 0), coef_ref, acc_ref, out_ref)
        for chunk in range(CHUNKS):
            add_chunk(t, chunk, obs_ref, face_ref, w_ref, acc_ref)
        return carry

    def pair(i, carry):
        return tile(2 * i + 1, tile(2 * i, carry))

    lax.fori_loop(0, tiles // 2, pair, 0)
    finish(tiles - 1, coef_ref, acc_ref, out_ref)


def partial_pressure(arrived, geom):
    tiles = arrived.shape[0]
    return pl.pallas_call(
        pressure_kernel,
        in_specs=[pl.BlockSpec(memory_space=pltpu.VMEM)] * 2,
        out_specs=pl.BlockSpec(memory_space=pltpu.VMEM),
        out_shape=jax.ShapeDtypeStruct((NFREQ, tiles, 4, PATCH), jnp.bfloat16),
        scratch_shapes=[
            pltpu.VMEM((tiles, 8, OBS_TILE), jnp.float32),
            pltpu.VMEM((tiles, TERMS, OBS_TILE), jnp.float32),
            pltpu.VMEM((8, FACES_OWN), jnp.float32),
            pltpu.VMEM((5, FACES_OWN, PATCH), jnp.float32),
            pltpu.VMEM((4 * FACES_OWN // PATCH, NFREQ * TERMS, PATCH), jnp.float32),
            pltpu.VMEM((CHUNKS, NFREQ, TERMS, 4 * CHUNK), jnp.bfloat16),
            pltpu.VMEM((NFREQ, TERMS, OBS_TILE), jnp.float32),
        ],
        compiler_params=pltpu.CompilerParams(vmem_limit_bytes=48 * 1024 * 1024),
        name="pressure",
    )(arrived, geom)


def local(signals, patch_count, patch_place, face_geom, obs_pos):
    owners = lax.axis_size("obs")
    groups = lax.axis_size("grp")
    outgoing = pack(signals, patch_count, patch_place, obs_pos, owners)
    arrived = lax.all_to_all(outgoing, "obs", split_axis=0, concat_axis=0, tiled=True)
    out = partial_pressure(arrived, face_geom)
    out = out.reshape(groups * owners, 4, PATCH)
    got = lax.all_to_all(out, ("grp", "obs"), split_axis=0, concat_axis=0, tiled=True)
    return jnp.sum(got.astype(jnp.float32), axis=0).reshape(2 * NFREQ // groups, OBS_TILE)


def solution(mesh):
    return jax.shard_map(
        local,
        mesh=mesh,
        in_specs=(
            P(None, None, ("grp", "obs")),
            P(("grp", "obs")),
            P(("grp", "obs")),
            P(None, ("grp", "obs")),
            P(None, "obs"),
        ),
        out_specs=P("grp", "obs"),
        check_vma=False,
    )
```

```python
import math

import jax
import jax.numpy as jnp
import numpy as np
from jax import lax
from jax.experimental import pallas as pl
from jax.experimental.pallas import tpu as pltpu
from jax.sharding import PartitionSpec as P

SAMPLES = 256
NFREQ = 8
NSIG = 4
PATCH = 128
MAXP = 8
PER_OWN = 4
FACES_OWN = 512
CHANNELS = NSIG * 2 * NFREQ
ROWS_MSG = 80
OBS_ROW = 64
OBS_TILE = 256
TERMS = 16
CHUNK = 64
CHUNKS = FACES_OWN // CHUNK
UNIT = 0.25 / math.pi
CENTER_X = 15.0

COS_COEFS = (
    0.9999992107823207,
    -19.73898035576387,
    64.92865742102978,
    -85.27162153426406,
    58.790492119980826,
    -21.071105627415147,
)
SIN_COEFS = (
    6.283184916495429,
    -41.34158923268831,
    81.59994332977428,
    -76.61447253115396,
    41.342882354135696,
    -12.471243534350362,
)


def spectral_basis():
    t = np.arange(SAMPLES, dtype=np.float64)
    m = np.arange(1, NFREQ + 1, dtype=np.float64)
    angles = 2.0 * math.pi / SAMPLES * (t[:, None] * m[None, :])
    window = (0.5 - 0.5 * np.cos(2.0 * math.pi / SAMPLES * t)) * math.sqrt(8.0 / (3.0 * SAMPLES))
    table = np.concatenate(
        [window[:, None] * np.cos(angles), -window[:, None] * np.sin(angles)], axis=1
    )
    return jnp.asarray(table.T.astype(np.float32)).astype(jnp.bfloat16)


def pack_kernel(
    count_hbm,
    place_hbm,
    basis_hbm,
    signals_hbm,
    obs_hbm,
    out_hbm,
    count_ref,
    place_ref,
    basis_ref,
    rows_ref,
    obs_ref,
    out_ref,
    sems,
    out_sems,
):
    reads = [
        pltpu.make_async_copy(src, dst, sems.at[n])
        for n, (src, dst) in enumerate(
            [
                (obs_hbm, obs_ref),
                (count_hbm, count_ref),
                (place_hbm, place_ref),
                (basis_hbm, basis_ref),
            ]
            + [(signals_hbm.at[s], rows_ref.at[s]) for s in range(NSIG)]
        )
    ]
    writes = []
    for n in range(NSIG + 1):
        rows = slice(n * 16, n * 16 + 16)
        writes.append(
            pltpu.make_async_copy(out_ref.at[:, rows, :], out_hbm.at[:, rows, :], out_sems.at[n])
        )
    for copy in reads:
        copy.start()
    for o in range(out_ref.shape[0]):
        out_ref[o, 0:CHANNELS, :] = jnp.zeros((CHANNELS, PATCH), jnp.bfloat16)
    reads[0].wait()
    x = obs_ref[...]
    hi = x.astype(jnp.bfloat16).astype(jnp.float32)
    rows = []
    for part in (hi, x - hi):
        for c in range(3):
            for h in range(2):
                rows.append(part[c : c + 1, h * PATCH : (h + 1) * PATCH])
    tail = jnp.concatenate(rows + [jnp.zeros((4, PATCH), jnp.float32)], axis=0)
    for o in range(out_ref.shape[0]):
        out_ref[o, OBS_ROW:, :] = tail.astype(jnp.bfloat16)
    row_id = lax.broadcasted_iota(jnp.int32, (16, PATCH), 0)
    reads[1].wait()
    reads[2].wait()
    count = count_ref[0, 0]
    for j in range(MAXP):
        place = place_ref[j]
        part_no = (place % PER_OWN + 1).astype(jnp.float32)

        @pl.when(j < count)
        def _():
            out_ref[place // PER_OWN, OBS_ROW:, :] = jnp.where(row_id < 12, tail, part_no).astype(
                jnp.bfloat16
            )

    writes[NSIG].start()
    reads[3].wait()
    for s in range(NSIG):
        reads[4 + s].wait()
        spec = jnp.dot(
            basis_ref[...], rows_ref[s], preferred_element_type=jnp.float32
        ).astype(jnp.bfloat16)
        for j in range(MAXP):

            @pl.when(j < count)
            def _():
                owner = place_ref[j] // PER_OWN
                out_ref[owner, s * 16 : s * 16 + 16, :] = spec[:, j * PATCH : (j + 1) * PATCH]

        writes[s].start()
    for copy in writes:
        copy.wait()


def pack(signals, patch_count, patch_place, obs_pos, owners):
    hbm = pl.BlockSpec(memory_space=pltpu.MemorySpace.HBM)
    shape = (owners, ROWS_MSG, PATCH)
    return pl.pallas_call(
        pack_kernel,
        in_specs=[hbm] * 5,
        out_specs=hbm,
        out_shape=jax.ShapeDtypeStruct(shape, jnp.bfloat16),
        scratch_shapes=[
            pltpu.SMEM((1, 1), jnp.int32),
            pltpu.SMEM((MAXP,), jnp.int32),
            pltpu.VMEM((2 * NFREQ, SAMPLES), jnp.bfloat16),
            pltpu.VMEM(signals.shape, signals.dtype),
            pltpu.VMEM(obs_pos.shape, obs_pos.dtype),
            pltpu.VMEM(shape, jnp.bfloat16),
            pltpu.SemaphoreType.DMA((NSIG + 4,)),
            pltpu.SemaphoreType.DMA((NSIG + 1,)),
        ],
        compiler_params=pltpu.CompilerParams(vmem_limit_bytes=67000000),
        name="pack",
    )(patch_count.reshape(1, 1), patch_place, spectral_basis(), signals, obs_pos)


def horner(coefs, z):
    acc = jnp.full_like(z, coefs[-1])
    for c in coefs[-2::-1]:
        acc = acc * z + c
    return acc


def add_chunk(t, chunk, obs_ref, face_ref, w_ref, acc_ref):
    state = []
    x = [obs_ref[t, c : c + 1, :] for c in range(4)]
    for group in range(CHUNK // 16):
        rows = slice(chunk * CHUNK + group * 16, chunk * CHUNK + group * 16 + 16)
        y = []
        for c in range(5):
            col = face_ref[c, rows, :]
            y.append(jnp.concatenate([col, col], axis=1))
        r2 = (x[3] + y[3]) + x[0] * y[0] + x[1] * y[1] + x[2] * y[2]
        inv = lax.rsqrt(r2)
        r = r2 * inv
        amp = y[4] * (inv * inv)
        frac = r - jnp.round(r)
        z = frac * frac
        cos1 = horner(COS_COEFS, z)
        sin1 = horner(SIN_COEFS, z) * frac
        state.append([cos1 + cos1, inv.astype(jnp.bfloat16), amp, amp * cos1, None, amp * sin1])
    for m in range(NFREQ):
        pieces = []
        for one in state:
            two_cos, other, c_old, c_now, s_old, s_now = one
            if m == 1:
                c_old, c_now = c_now, two_cos * c_now - c_old
                s_old, s_now = s_now, two_cos * s_now
            elif m > 1:
                c_old, c_now = c_now, two_cos * c_now - c_old
                s_old, s_now = s_now, two_cos * s_now - s_old
            one[2:] = [c_old, c_now, s_old, s_now]
            c_half, s_half = c_now.astype(jnp.bfloat16), s_now.astype(jnp.bfloat16)
            pieces.append((c_half, s_half, c_half * other, s_half * other))
        g = jnp.concatenate([p[family] for family in range(4) for p in pieces], axis=0)
        part = jnp.dot(w_ref[chunk, m], g, preferred_element_type=jnp.float32)
        acc_ref[m] = part if chunk == 0 else acc_ref[m] + part


def finish(t, coef_ref, accs, out_ref):
    coef = coef_ref[t]
    for pair in range(NFREQ // 2):
        lines = ([], [])
        for m in (2 * pair, 2 * pair + 1):
            terms = accs[m] * coef
            value = terms[0:8] + terms[8:16]
            value = value + pltpu.roll(value, 4, axis=0)
            value = value + pltpu.roll(value, 2, axis=0)
            value = value * (0.5 * (m + 1) / (16.0 * math.pi**2))
            for part in range(2):
                row = value[part : part + 1]
                lines[part].extend([row[:, 0:PATCH], row[:, PATCH:]])
        for part in range(2):
            block = jnp.concatenate(lines[part], axis=0)
            out_ref[part * (NFREQ // 2) + pair, t] = block.astype(out_ref.dtype)


def build_observers(arrived_ref, obs_ref, coef_ref):
    for t in range(arrived_ref.shape[0]):
        rows = arrived_ref[t, OBS_ROW : OBS_ROW + 16, :].astype(jnp.float32)
        pos = rows[0:6] + rows[6:12]
        for c in range(3):
            line = jnp.concatenate([pos[2 * c : 2 * c + 1], pos[2 * c + 1 : 2 * c + 2]], axis=1)
            line = (line - CENTER_X if c == 0 else line) * UNIT
            obs_ref[t, c : c + 1, :] = line
        x = [obs_ref[t, c : c + 1, :] for c in range(3)]
        xx = x[0] * x[0] + x[1] * x[1] + x[2] * x[2]
        obs_ref[t, 3:4, :] = xx
        one = jnp.ones_like(xx)
        for n, row in enumerate((xx, one, one, x[0], x[1], x[2], x[0], x[1])):
            coef_ref[t, 2 * n : 2 * n + 2, :] = jnp.broadcast_to(row, (2, OBS_TILE))


def build_faces(geom_ref, geo_ref, face_ref):
    geo_ref[0:1, :] = (geom_ref[0:1, :] - CENTER_X) * UNIT
    geo_ref[1:3, :] = geom_ref[1:3, :] * UNIT
    y = [geo_ref[c : c + 1, :] for c in range(3)]
    for c in range(3):
        geo_ref[4 + c : 5 + c, :] = -2.0 * y[c]
    geo_ref[3:4, :] = y[0] * y[0] + y[1] * y[1] + y[2] * y[2]
    geo_ref[7:8, :] = geom_ref[3:4, :]
    cols = geo_ref[...].T
    for c, row in enumerate((4, 5, 6, 3, 7)):
        face_ref[c] = jnp.broadcast_to(cols[:, row : row + 1], (FACES_OWN, PATCH))


def build_weights(arrived_ref, geo_ref, wide_ref, w_ref):
    inv_k = 1.0 / (
        2.0
        * math.pi
        * (1 + lax.broadcasted_iota(jnp.int32, (NFREQ, PATCH), 0)).astype(jnp.float32)
    )
    left = lax.broadcasted_iota(jnp.int32, (NFREQ, PATCH), 1) < CHUNK
    for j in range(PER_OWN):
        spec = jnp.zeros((CHANNELS, PATCH), jnp.float32)
        for o in range(arrived_ref.shape[0]):
            tail = arrived_ref[o, OBS_ROW : OBS_ROW + 16, :].astype(jnp.float32)
            picked = (tail[15:16, :] == float(j + 1)).astype(jnp.float32)
            spec = spec + arrived_ref[o, 0:CHANNELS, :].astype(jnp.float32) * picked
        y = [geo_ref[c : c + 1, j * PATCH : (j + 1) * PATCH] for c in range(3)]
        yy = geo_ref[3:4, j * PATCH : (j + 1) * PATCH]
        qr, qi = spec[0:8], spec[8:16]
        lr = [spec[16 + 16 * c : 24 + 16 * c] for c in range(3)]
        li = [spec[24 + 16 * c : 32 + 16 * c] for c in range(3)]
        lyr = lr[0] * y[0] + lr[1] * y[1] + lr[2] * y[2]
        lyi = li[0] * y[0] + li[1] * y[1] + li[2] * y[2]
        zero = jnp.zeros_like(qr)

        def four(load_r, load_i, mono):
            near_r, near_i = load_r * inv_k, load_i * inv_k
            mono_r, mono_i = mono * qr, mono * qi
            return (
                (-load_i, load_r, near_r - mono_i, near_i + mono_r),
                (load_r, load_i, near_i + mono_r, mono_i - near_r),
            )

        def put(term, values):
            for pair in range(2):
                a, b = values[2 * pair], values[2 * pair + 1]
                first = jnp.where(left, a, pltpu.roll(b, CHUNK, axis=1))
                second = jnp.where(left, pltpu.roll(a, CHUNK, axis=1), b)
                rows = pl.ds(term, NFREQ, stride=TERMS)
                wide_ref[4 * j + pair, rows, :] = first
                wide_ref[4 * j + 2 + pair, rows, :] = second

        square = ((zero, zero, -qi, qr), (zero, zero, qr, qi))
        base = four(-lyr, -lyi, yy)
        load = [four(lr[c], li[c], -2.0 * y[c]) for c in range(3)]
        def split(values):
            hi = [v.astype(jnp.bfloat16).astype(jnp.float32) for v in values]
            return hi, [v - h for v, h in zip(values, hi)]

        for part in range(2):
            put(part, square[part])
            hi, low = split(base[part])
            put(2 + part, hi)
            put(4 + part, low)
            for c in range(3):
                hi, low = split(load[c][part])
                put(6 + 2 * c + part, hi)
                if c < 2:
                    put(12 + 2 * c + part, low)
    for chunk in range(CHUNKS):
        for m in range(NFREQ):
            for side in range(2):
                w_ref[chunk, m, :, side * PATCH : (side + 1) * PATCH] = wide_ref[
                    2 * chunk + side, m * TERMS : (m + 1) * TERMS, :
                ].astype(jnp.bfloat16)


def pressure_kernel(
    arrived_ref, geom_ref, out_ref, obs_ref, coef_ref, geo_ref, face_ref, wide_ref, w_ref, acc_ref
):
    tiles = arrived_ref.shape[0]
    build_observers(arrived_ref, obs_ref, coef_ref)
    build_faces(geom_ref, geo_ref, face_ref)
    build_weights(arrived_ref, geo_ref, wide_ref, w_ref)

    def tile(t, carry):
        finish(jnp.maximum(t - 1, 0), coef_ref, acc_ref, out_ref)
        for chunk in range(CHUNKS):
            add_chunk(t, chunk, obs_ref, face_ref, w_ref, acc_ref)
        return carry

    def pair(i, carry):
        for n in range(4):
            carry = tile(4 * i + n, carry)
        return carry

    lax.fori_loop(0, tiles // 4, pair, 0)
    finish(tiles - 1, coef_ref, acc_ref, out_ref)


def partial_pressure(arrived, geom):
    tiles = arrived.shape[0]
    return pl.pallas_call(
        pressure_kernel,
        in_specs=[pl.BlockSpec(memory_space=pltpu.VMEM)] * 2,
        out_specs=pl.BlockSpec(memory_space=pltpu.VMEM),
        out_shape=jax.ShapeDtypeStruct((NFREQ, tiles, 4, PATCH), jnp.bfloat16),
        scratch_shapes=[
            pltpu.VMEM((tiles, 8, OBS_TILE), jnp.float32),
            pltpu.VMEM((tiles, TERMS, OBS_TILE), jnp.float32),
            pltpu.VMEM((8, FACES_OWN), jnp.float32),
            pltpu.VMEM((5, FACES_OWN, PATCH), jnp.float32),
            pltpu.VMEM((4 * FACES_OWN // PATCH, NFREQ * TERMS, PATCH), jnp.float32),
            pltpu.VMEM((CHUNKS, NFREQ, TERMS, 4 * CHUNK), jnp.bfloat16),
            pltpu.VMEM((NFREQ, TERMS, OBS_TILE), jnp.float32),
        ],
        compiler_params=pltpu.CompilerParams(vmem_limit_bytes=48 * 1024 * 1024),
        name="pressure",
    )(arrived, geom)


def local(signals, patch_count, patch_place, face_geom, obs_pos):
    owners = lax.axis_size("obs")
    groups = lax.axis_size("grp")
    outgoing = pack(signals, patch_count, patch_place, obs_pos, owners)
    arrived = lax.all_to_all(outgoing, "obs", split_axis=0, concat_axis=0, tiled=True)
    out = partial_pressure(arrived, face_geom)
    out = out.reshape(groups * owners, 4, PATCH)
    got = lax.all_to_all(out, ("grp", "obs"), split_axis=0, concat_axis=0, tiled=True)
    return jnp.sum(got.astype(jnp.float32), axis=0).reshape(2 * NFREQ // groups, OBS_TILE)


def solution(mesh):
    return jax.shard_map(
        local,
        mesh=mesh,
        in_specs=(
            P(None, None, ("grp", "obs")),
            P(("grp", "obs")),
            P(("grp", "obs")),
            P(None, ("grp", "obs")),
            P(None, "obs"),
        ),
        out_specs=P("grp", "obs"),
        check_vma=False,
    )
```

```python
import math

import jax
import jax.numpy as jnp
import numpy as np
from jax import lax
from jax.experimental import pallas as pl
from jax.experimental.pallas import tpu as pltpu
from jax.sharding import PartitionSpec as P

SAMPLES = 256
NFREQ = 8
NSIG = 4
PATCH = 128
MAXP = 8
PER_OWN = 4
FACES_OWN = 512
CHANNELS = NSIG * 2 * NFREQ
ROWS_MSG = 80
OBS_ROW = 64
OBS_TILE = 256
TERMS = 16
CHUNK = 64
CHUNKS = FACES_OWN // CHUNK
UNIT = 0.25 / math.pi
CENTER_X = 15.0

COS_COEFS = (
    0.9999992107823207,
    -19.73898035576387,
    64.92865742102978,
    -85.27162153426406,
    58.790492119980826,
    -21.071105627415147,
)
SIN_COEFS = (
    6.283184916495429,
    -41.34158923268831,
    81.59994332977428,
    -76.61447253115396,
    41.342882354135696,
    -12.471243534350362,
)


def spectral_basis():
    t = np.arange(SAMPLES, dtype=np.float64)
    m = np.arange(1, NFREQ + 1, dtype=np.float64)
    angles = 2.0 * math.pi / SAMPLES * (t[:, None] * m[None, :])
    window = (0.5 - 0.5 * np.cos(2.0 * math.pi / SAMPLES * t)) * math.sqrt(8.0 / (3.0 * SAMPLES))
    table = np.concatenate(
        [window[:, None] * np.cos(angles), -window[:, None] * np.sin(angles)], axis=1
    )
    return jnp.asarray(table.T.astype(np.float32)).astype(jnp.bfloat16)


def pack_kernel(
    count_hbm,
    place_hbm,
    basis_hbm,
    signals_hbm,
    obs_hbm,
    out_hbm,
    count_ref,
    place_ref,
    basis_ref,
    rows_ref,
    obs_ref,
    out_ref,
    sems,
    out_sems,
):
    reads = [
        pltpu.make_async_copy(src, dst, sems.at[n])
        for n, (src, dst) in enumerate(
            [
                (obs_hbm, obs_ref),
                (count_hbm, count_ref),
                (place_hbm, place_ref),
                (basis_hbm, basis_ref),
            ]
            + [(signals_hbm.at[s], rows_ref.at[s]) for s in range(NSIG)]
        )
    ]
    writes = []
    for n in range(NSIG + 1):
        rows = slice(n * 16, n * 16 + 16)
        writes.append(
            pltpu.make_async_copy(out_ref.at[:, rows, :], out_hbm.at[:, rows, :], out_sems.at[n])
        )
    for copy in reads:
        copy.start()
    for o in range(out_ref.shape[0]):
        out_ref[o, 0:CHANNELS, :] = jnp.zeros((CHANNELS, PATCH), jnp.bfloat16)
    reads[0].wait()
    x = obs_ref[...]
    hi = x.astype(jnp.bfloat16).astype(jnp.float32)
    rows = []
    for part in (hi, x - hi):
        for c in range(3):
            for h in range(2):
                rows.append(part[c : c + 1, h * PATCH : (h + 1) * PATCH])
    tail = jnp.concatenate(rows + [jnp.zeros((4, PATCH), jnp.float32)], axis=0)
    for o in range(out_ref.shape[0]):
        out_ref[o, OBS_ROW:, :] = tail.astype(jnp.bfloat16)
    row_id = lax.broadcasted_iota(jnp.int32, (16, PATCH), 0)
    reads[1].wait()
    reads[2].wait()
    count = count_ref[0, 0]
    for j in range(MAXP):
        place = place_ref[j]
        part_no = (place % PER_OWN + 1).astype(jnp.float32)

        @pl.when(j < count)
        def _():
            out_ref[place // PER_OWN, OBS_ROW:, :] = jnp.where(row_id < 12, tail, part_no).astype(
                jnp.bfloat16
            )

    writes[NSIG].start()
    reads[3].wait()
    for s in range(NSIG):
        reads[4 + s].wait()
        spec = jnp.dot(
            basis_ref[...], rows_ref[s], preferred_element_type=jnp.float32
        ).astype(jnp.bfloat16)
        for j in range(MAXP):

            @pl.when(j < count)
            def _():
                owner = place_ref[j] // PER_OWN
                out_ref[owner, s * 16 : s * 16 + 16, :] = spec[:, j * PATCH : (j + 1) * PATCH]

        writes[s].start()
    for copy in writes:
        copy.wait()


def pack(signals, patch_count, patch_place, obs_pos, owners):
    hbm = pl.BlockSpec(memory_space=pltpu.MemorySpace.HBM)
    shape = (owners, ROWS_MSG, PATCH)
    return pl.pallas_call(
        pack_kernel,
        in_specs=[hbm] * 5,
        out_specs=hbm,
        out_shape=jax.ShapeDtypeStruct(shape, jnp.bfloat16),
        scratch_shapes=[
            pltpu.SMEM((1, 1), jnp.int32),
            pltpu.SMEM((MAXP,), jnp.int32),
            pltpu.VMEM((2 * NFREQ, SAMPLES), jnp.bfloat16),
            pltpu.VMEM(signals.shape, signals.dtype),
            pltpu.VMEM(obs_pos.shape, obs_pos.dtype),
            pltpu.VMEM(shape, jnp.bfloat16),
            pltpu.SemaphoreType.DMA((NSIG + 4,)),
            pltpu.SemaphoreType.DMA((NSIG + 1,)),
        ],
        compiler_params=pltpu.CompilerParams(vmem_limit_bytes=67000000),
        name="pack",
    )(patch_count.reshape(1, 1), patch_place, spectral_basis(), signals, obs_pos)


def horner(coefs, z):
    acc = jnp.full_like(z, coefs[-1])
    for c in coefs[-2::-1]:
        acc = acc * z + c
    return acc


def add_chunk(t, chunk, obs_ref, face_ref, w_ref, acc_ref):
    state = []
    x = [obs_ref[t, c : c + 1, :] for c in range(4)]
    for group in range(CHUNK // 16):
        rows = slice(chunk * CHUNK + group * 16, chunk * CHUNK + group * 16 + 16)
        y = []
        for c in range(5):
            col = face_ref[c, rows, :]
            y.append(jnp.concatenate([col, col], axis=1))
        r2 = (x[3] + y[3]) + x[0] * y[0] + x[1] * y[1] + x[2] * y[2]
        inv = lax.rsqrt(r2)
        r = r2 * inv
        amp = y[4] * (inv * inv)
        frac = r - jnp.round(r)
        z = frac * frac
        cos1 = horner(COS_COEFS, z)
        sin1 = horner(SIN_COEFS, z) * frac
        state.append([cos1 + cos1, inv.astype(jnp.bfloat16), amp, amp * cos1, None, amp * sin1])
    for m in range(NFREQ):
        pieces = []
        for one in state:
            two_cos, other, c_old, c_now, s_old, s_now = one
            if m == 1:
                c_old, c_now = c_now, two_cos * c_now - c_old
                s_old, s_now = s_now, two_cos * s_now
            elif m > 1:
                c_old, c_now = c_now, two_cos * c_now - c_old
                s_old, s_now = s_now, two_cos * s_now - s_old
            one[2:] = [c_old, c_now, s_old, s_now]
            c_half, s_half = c_now.astype(jnp.bfloat16), s_now.astype(jnp.bfloat16)
            pieces.append((c_half, s_half, c_half * other, s_half * other))
        g = jnp.concatenate([p[family] for family in range(4) for p in pieces], axis=0)
        part = jnp.dot(w_ref[chunk, m], g, preferred_element_type=jnp.float32)
        acc_ref[m] = part if chunk == 0 else acc_ref[m] + part


def finish(t, coef_ref, accs, out_ref):
    coef = coef_ref[t]
    for pair in range(NFREQ // 2):
        lines = ([], [])
        for m in (2 * pair, 2 * pair + 1):
            terms = accs[m] * coef
            value = terms[0:8] + terms[8:16]
            value = value + pltpu.roll(value, 4, axis=0)
            value = value + pltpu.roll(value, 2, axis=0)
            value = value * (0.5 * (m + 1) / (16.0 * math.pi**2))
            for part in range(2):
                row = value[part : part + 1]
                lines[part].extend([row[:, 0:PATCH], row[:, PATCH:]])
        for part in range(2):
            block = jnp.concatenate(lines[part], axis=0)
            out_ref[part * (NFREQ // 2) + pair, t] = block.astype(out_ref.dtype)


def build_observers(arrived_ref, obs_ref, coef_ref):
    for t in range(arrived_ref.shape[0]):
        rows = arrived_ref[t, OBS_ROW : OBS_ROW + 16, :].astype(jnp.float32)
        pos = rows[0:6] + rows[6:12]
        for c in range(3):
            line = jnp.concatenate([pos[2 * c : 2 * c + 1], pos[2 * c + 1 : 2 * c + 2]], axis=1)
            line = (line - CENTER_X if c == 0 else line) * UNIT
            obs_ref[t, c : c + 1, :] = line
        x = [obs_ref[t, c : c + 1, :] for c in range(3)]
        xx = x[0] * x[0] + x[1] * x[1] + x[2] * x[2]
        obs_ref[t, 3:4, :] = xx
        one = jnp.ones_like(xx)
        for n, row in enumerate((xx, one, one, x[0], x[1], x[2], x[0], x[1])):
            coef_ref[t, 2 * n : 2 * n + 2, :] = jnp.broadcast_to(row, (2, OBS_TILE))


def build_faces(geom_ref, geo_ref, face_ref):
    geo_ref[0:1, :] = (geom_ref[0:1, :] - CENTER_X) * UNIT
    geo_ref[1:3, :] = geom_ref[1:3, :] * UNIT
    y = [geo_ref[c : c + 1, :] for c in range(3)]
    for c in range(3):
        geo_ref[4 + c : 5 + c, :] = -2.0 * y[c]
    geo_ref[3:4, :] = y[0] * y[0] + y[1] * y[1] + y[2] * y[2]
    geo_ref[7:8, :] = geom_ref[3:4, :]
    cols = geo_ref[...].T
    for c, row in enumerate((4, 5, 6, 3, 7)):
        face_ref[c] = jnp.broadcast_to(cols[:, row : row + 1], (FACES_OWN, PATCH))


def build_weights(arrived_ref, geo_ref, wide_ref, w_ref):
    inv_k = 1.0 / (
        2.0
        * math.pi
        * (1 + lax.broadcasted_iota(jnp.int32, (NFREQ, PATCH), 0)).astype(jnp.float32)
    )
    left = lax.broadcasted_iota(jnp.int32, (NFREQ, PATCH), 1) < CHUNK
    for j in range(PER_OWN):
        spec = jnp.zeros((CHANNELS, PATCH), jnp.float32)
        for o in range(arrived_ref.shape[0]):
            tail = arrived_ref[o, OBS_ROW : OBS_ROW + 16, :].astype(jnp.float32)
            picked = (tail[15:16, :] == float(j + 1)).astype(jnp.float32)
            spec = spec + arrived_ref[o, 0:CHANNELS, :].astype(jnp.float32) * picked
        y = [geo_ref[c : c + 1, j * PATCH : (j + 1) * PATCH] for c in range(3)]
        yy = geo_ref[3:4, j * PATCH : (j + 1) * PATCH]
        qr, qi = spec[0:8], spec[8:16]
        lr = [spec[16 + 16 * c : 24 + 16 * c] for c in range(3)]
        li = [spec[24 + 16 * c : 32 + 16 * c] for c in range(3)]
        lyr = lr[0] * y[0] + lr[1] * y[1] + lr[2] * y[2]
        lyi = li[0] * y[0] + li[1] * y[1] + li[2] * y[2]
        zero = jnp.zeros_like(qr)

        def four(load_r, load_i, mono):
            near_r, near_i = load_r * inv_k, load_i * inv_k
            mono_r, mono_i = mono * qr, mono * qi
            return (
                (-load_i, load_r, near_r - mono_i, near_i + mono_r),
                (load_r, load_i, near_i + mono_r, mono_i - near_r),
            )

        def put(term, values):
            for pair in range(2):
                a, b = values[2 * pair], values[2 * pair + 1]
                first = jnp.where(left, a, pltpu.roll(b, CHUNK, axis=1))
                second = jnp.where(left, pltpu.roll(a, CHUNK, axis=1), b)
                rows = pl.ds(term, NFREQ, stride=TERMS)
                wide_ref[4 * j + pair, rows, :] = first
                wide_ref[4 * j + 2 + pair, rows, :] = second

        square = ((zero, zero, -qi, qr), (zero, zero, qr, qi))
        base = four(-lyr, -lyi, yy)
        load = [four(lr[c], li[c], -2.0 * y[c]) for c in range(3)]
        def split(values):
            hi = [v.astype(jnp.bfloat16).astype(jnp.float32) for v in values]
            return hi, [v - h for v, h in zip(values, hi)]

        for part in range(2):
            put(part, square[part])
            hi, low = split(base[part])
            put(2 + part, hi)
            put(4 + part, low)
            for c in range(3):
                hi, low = split(load[c][part])
                put(6 + 2 * c + part, hi)
                if c < 2:
                    put(12 + 2 * c + part, low)
    for chunk in range(CHUNKS):
        for m in range(NFREQ):
            for side in range(2):
                w_ref[chunk, m, :, side * PATCH : (side + 1) * PATCH] = wide_ref[
                    2 * chunk + side, m * TERMS : (m + 1) * TERMS, :
                ].astype(jnp.bfloat16)


def pressure_kernel(
    arrived_ref, geom_ref, out_ref, obs_ref, coef_ref, geo_ref, face_ref, wide_ref, w_ref, acc_ref
):
    tiles = arrived_ref.shape[0]
    build_observers(arrived_ref, obs_ref, coef_ref)
    build_faces(geom_ref, geo_ref, face_ref)
    build_weights(arrived_ref, geo_ref, wide_ref, w_ref)

    def tile(t, carry):
        finish(jnp.maximum(t - 1, 0), coef_ref, acc_ref, out_ref)
        for chunk in range(CHUNKS):
            add_chunk(t, chunk, obs_ref, face_ref, w_ref, acc_ref)
        return carry

    def pair(i, carry):
        for n in range(8):
            carry = tile(8 * i + n, carry)
        return carry

    lax.fori_loop(0, tiles // 8, pair, 0)
    finish(tiles - 1, coef_ref, acc_ref, out_ref)


def partial_pressure(arrived, geom):
    tiles = arrived.shape[0]
    return pl.pallas_call(
        pressure_kernel,
        in_specs=[pl.BlockSpec(memory_space=pltpu.VMEM)] * 2,
        out_specs=pl.BlockSpec(memory_space=pltpu.VMEM),
        out_shape=jax.ShapeDtypeStruct((NFREQ, tiles, 4, PATCH), jnp.bfloat16),
        scratch_shapes=[
            pltpu.VMEM((tiles, 8, OBS_TILE), jnp.float32),
            pltpu.VMEM((tiles, TERMS, OBS_TILE), jnp.float32),
            pltpu.VMEM((8, FACES_OWN), jnp.float32),
            pltpu.VMEM((5, FACES_OWN, PATCH), jnp.float32),
            pltpu.VMEM((4 * FACES_OWN // PATCH, NFREQ * TERMS, PATCH), jnp.float32),
            pltpu.VMEM((CHUNKS, NFREQ, TERMS, 4 * CHUNK), jnp.bfloat16),
            pltpu.VMEM((NFREQ, TERMS, OBS_TILE), jnp.float32),
        ],
        compiler_params=pltpu.CompilerParams(vmem_limit_bytes=48 * 1024 * 1024),
        name="pressure",
    )(arrived, geom)


def local(signals, patch_count, patch_place, face_geom, obs_pos):
    owners = lax.axis_size("obs")
    groups = lax.axis_size("grp")
    outgoing = pack(signals, patch_count, patch_place, obs_pos, owners)
    arrived = lax.all_to_all(outgoing, "obs", split_axis=0, concat_axis=0, tiled=True)
    out = partial_pressure(arrived, face_geom)
    out = out.reshape(groups * owners, 4, PATCH)
    got = lax.all_to_all(out, ("grp", "obs"), split_axis=0, concat_axis=0, tiled=True)
    return jnp.sum(got.astype(jnp.float32), axis=0).reshape(2 * NFREQ // groups, OBS_TILE)


def solution(mesh):
    return jax.shard_map(
        local,
        mesh=mesh,
        in_specs=(
            P(None, None, ("grp", "obs")),
            P(("grp", "obs")),
            P(("grp", "obs")),
            P(None, ("grp", "obs")),
            P(None, "obs"),
        ),
        out_specs=P("grp", "obs"),
        check_vma=False,
    )
```
